128 devices in a mesh: view: 4 (over z), seg: 32 (over x, y, core).
Axes of the slice: x: 4, y: 4, z: 4, core: 2. Of those that a mesh axis runs over, the one named last changes fastest.
Arguments:
- features: bfloat16 [128, 1369, 1024], P(('view', 'seg')), may hold values from -6 to 6
- block_ids: int32 [128, 32, 2], P(('view', 'seg')), may hold values from 0 to 32, as said below
- patch_rows: int32 [128, 32, 2, 32], P(('view', 'seg')), may hold values from 0 to 1368
- lift_weights: bfloat16 [128, 32, 2, 64, 32], P(('view', 'seg')), may hold values from 0 to 0.5
- coords: int32 [4, 32, 3, 512], P('view', 'seg'), may hold values from 0 to 127, as said below
- w_in: float32 [1024, 768], replicated, may hold values from -0.1875 to 0.1875
- w_query: bfloat16 [768, 768], replicated, may hold values from -1 to 1
- w_key: bfloat16 [768, 768], replicated, may hold values from -1 to 1
- w_value: bfloat16 [768, 768], replicated, may hold values from -0.21875 to 0.21875
- w_out: bfloat16 [768, 768], replicated, may hold values from -0.21875 to 0.21875
- w_up: bfloat16 [768, 3072], replicated, may hold values from -0.21875 to 0.21875
- w_down: bfloat16 [3072, 768], replicated, may hold values from -0.109375 to 0.109375
Outputs:
- encoded: bfloat16 [4, 32, 512, 768], P('view', 'seg')
The draws below stay inside these ranges and needn't reach their ends.
Inputs may be any that keep to these rules, and one draw needn't show every extreme that they name: In each row block_ids[j, s] the live entries (below 32) come first, are distinct and number 1 to 2; the others equal 32. All rows of one destination segment are full. The value 4 * 8 - 1 never occurs. `coords`: the three coordinates of distinct voxels of a 128-cube; their Morton codes rise strictly with the voxel index.
All inputs are finite; a program needn't handle non-finite values.
Results may differ from the reference program's by a relative error of at most 0.007.
Values may be sent and summed in bfloat16 or wider, within the bound.
No kernel may reach another device: no remote copies, remote signals or barrier semaphores. Data moves between devices by JAX's collectives and lax.ppermute only.
A program may use at most 128 MiB of HBM per device.

```python
import math
import jax
import jax.numpy as jnp
from jax import lax

C = 1024
D = 768
HEADS = 12
HEAD_DIM = 64
FF = 3072
PATCHES = 1369
BLOCK_PATCHES = 32
BLOCK = 64
CAP = 2
ROWS_DEV = 512
VIEWS = 128
N_VIEW = 4
N_SEG = 32


def draw_block_ids(key, part):
    segment_blocks = N_VIEW * (ROWS_DEV // BLOCK)
    base_key = jax.random.fold_in(key, 11)
    key_scores, key_live, key_full = jax.random.split(base_key, 3)
    scores = jax.random.randint(key_scores, (VIEWS, N_SEG, segment_blocks - 1), 0, 1 << 20)
    scores = scores * (segment_blocks - 1) + jnp.arange(segment_blocks - 1, dtype=jnp.int32)
    order = jnp.argsort(scores, axis=-1)[..., :CAP].astype(jnp.int32)
    live = jax.random.randint(key_live, (VIEWS, N_SEG, 1), 1, CAP + 1)
    full_segment = jax.random.randint(key_full, (), 0, N_SEG)
    live = jnp.where(jnp.arange(N_SEG, dtype=jnp.int32)[None, :, None] == full_segment, CAP, live)
    slot_index = jnp.arange(CAP, dtype=jnp.int32)
    return jnp.where(slot_index < live, order, segment_blocks).astype(jnp.int32)


def draw_coords(key, part):
    voxel_count = N_VIEW * N_SEG * ROWS_DEV
    steps_between = jax.random.randint(jax.random.fold_in(key, 23), (voxel_count,), 1, 8)
    codes = jnp.cumsum(steps_between) - steps_between[0]
    codes = codes.at[-1].set(2097151)
    axes_out = []
    for axis_pos in range(3):
        coordinate = jnp.zeros_like(codes)
        for bit_pos in range(7):
            coordinate = coordinate + codes // (1 << 3 * bit_pos + axis_pos) % 2 * (1 << bit_pos)
        axes_out.append(coordinate)
    stacked = jnp.stack(axes_out, axis=0).reshape(3, N_VIEW, N_SEG, ROWS_DEV)
    return jnp.transpose(stacked, (1, 2, 0, 3)).astype(jnp.int32)


def attention_pair(key):
    base_key = jax.random.fold_in(key, 31)
    key_query = jax.random.fold_in(base_key, 2)
    key_extra = jax.random.fold_in(base_key, 3)
    spread = 1.0 / math.sqrt(D)
    query_part = jax.random.normal(key_query, (D, D), jnp.float32) * spread
    key_part = jax.random.normal(key_extra, (D, D), jnp.float32) * spread
    return (jnp.clip(query_part, -1.0, 1.0), jnp.clip(key_part, -1.0, 1.0))


def draw_w_query(key, part):
    return attention_pair(key)[0].astype(jnp.bfloat16)


def draw_w_key(key, part):
    return attention_pair(key)[1].astype(jnp.bfloat16)


def plant(result, rng, smallest, high):
    longest = result.shape.index(max(result.shape))
    spots = []
    for shift in (0, 1):
        where = [jax.random.randint(jax.random.fold_in(rng, axis), (), 0, length) for axis, length in enumerate(result.shape)]
        where[longest] = (where[longest] + shift) % result.shape[longest]
        spots.append(tuple(where))
    return result.at[spots[0]].set(smallest).at[spots[1]].set(high)


def levels(own_key, dims, cuts, least, high):
    level, own = 1.0, jax.random.fold_in(own_key, 6)
    for dim, parts in cuts:
        steps = jnp.exp(jax.random.uniform(jax.random.fold_in(own, dim), (parts,), jnp.float32, least / len(cuts), high / len(cuts)))
        level = level * jnp.repeat(steps, dims[dim] // parts).reshape([-1 if axis == dim else 1 for axis in range(len(dims))])
    return level


def scatter_about(rng, extent, scale, bound, cuts=(), kind=jnp.bfloat16):
    gain = levels(rng, extent, cuts, -0.22, 0.18) if cuts else 1.0
    entries = jax.random.normal(rng, extent, jnp.float32) * scale * gain
    return jnp.minimum(jnp.maximum(entries, -bound), bound).astype(kind)


def setup_inputs(seed: int = 0) -> dict:
    splits = jax.random.split(jax.random.key(seed), 13)
    return {
        "features": scatter_about(splits[0], (VIEWS, PATCHES, C), 1.0, 6.0, ((0, 128),)),
        "block_ids": draw_block_ids(jax.random.fold_in(splits[12], 71), 0),
        "patch_rows": plant(jax.random.randint(splits[2], (VIEWS, N_SEG, CAP, BLOCK_PATCHES), 0, PATCHES), jax.random.fold_in(splits[2], 1), 0, PATCHES - 1).astype(jnp.int32),
        "lift_weights": jnp.clip(0.5 * jax.random.uniform(splits[3], (VIEWS, N_SEG, CAP, BLOCK, BLOCK_PATCHES), jnp.float32) ** levels(splits[3], (VIEWS, N_SEG, CAP, BLOCK, BLOCK_PATCHES), ((0, 128),), -0.2, 0.2), 0.0, 0.5).astype(jnp.bfloat16),
        "coords": draw_coords(jax.random.fold_in(splits[12], 71), 0),
        "w_in": scatter_about(splits[5], (C, D), C ** -0.5, 0.1875, (), jnp.float32),
        "w_query": draw_w_query(jax.random.fold_in(splits[12], 71), 0),
        "w_key": draw_w_key(jax.random.fold_in(splits[12], 71), 0),
        "w_value": scatter_about(splits[8], (D, D), D ** -0.5, 0.21875),
        "w_out": scatter_about(splits[9], (D, D), D ** -0.5, 0.21875),
        "w_up": scatter_about(splits[10], (D, FF), D ** -0.5, 0.21875),
        "w_down": scatter_about(splits[11], (FF, D), FF ** -0.5, 0.109375),
    }


def normalize(values):
    average = lax.optimization_barrier(jnp.mean(values, axis=-1, keepdims=True))
    centred = values - average
    spread = lax.optimization_barrier(jnp.mean(centred * centred, axis=-1, keepdims=True))
    return (centred * lax.rsqrt(spread + 1e-05)).astype(jnp.bfloat16)

def position_code(places, model_width):
    freq_count = model_width // 6
    frequency = jnp.exp(-math.log(10000.0) * jnp.arange(freq_count, dtype=jnp.float32) / freq_count)
    angles = places.astype(jnp.float32)[:, :, None] * frequency
    pieces = jnp.concatenate([jnp.sin(angles), jnp.cos(angles)], axis=-1)
    return jnp.transpose(pieces, (1, 0, 2)).reshape(places.shape[1], model_width)

def reference(features, block_ids, patch_rows, lift_weights, coords, w_in, w_query, w_key, w_value, w_out, w_up, w_down):
    quarter_blocks = ROWS_DEV // BLOCK
    segment_blocks = N_VIEW * quarter_blocks
    channel_count = features.shape[-1]
    voxel_count = N_VIEW * N_SEG * ROWS_DEV
    segment_index = jnp.arange(N_SEG, dtype=jnp.int32)[:, None]

    def add_view(carry, inputs):
        sums, tallies = carry
        view_table, view_ids, view_rows, view_weights = inputs
        patches = view_table[view_rows].astype(jnp.float32)
        lifted = jnp.einsum('sabk,sakc->sabc', view_weights.astype(jnp.float32), patches).astype(jnp.bfloat16)
        lifted = lax.optimization_barrier(lifted).astype(jnp.float32)
        sums = sums.at[segment_index, view_ids].add(lifted)
        tallies = tallies.at[segment_index, view_ids].add(jnp.ones(view_ids.shape, jnp.float32))
        return ((sums, tallies), None)
    start = (jnp.zeros((N_SEG, segment_blocks + 1, BLOCK, channel_count), jnp.float32), jnp.zeros((N_SEG, segment_blocks + 1), jnp.float32))
    (sums, tallies), _ = lax.scan(add_view, start, (features, block_ids, patch_rows, lift_weights))
    sums = sums[:, :segment_blocks].reshape(N_SEG, N_VIEW, quarter_blocks * BLOCK, channel_count)
    sums = jnp.transpose(sums, (1, 0, 2, 3)).reshape(voxel_count, channel_count)
    tallies = tallies[:, :segment_blocks].reshape(N_SEG, N_VIEW, quarter_blocks)
    tallies = jnp.transpose(tallies, (1, 0, 2)).reshape(-1)
    projected = jnp.dot(sums, w_in, precision=lax.Precision.HIGHEST, preferred_element_type=jnp.float32)
    model_width = projected.shape[1]
    averaged = (projected.reshape(-1, BLOCK, model_width) / jnp.maximum(tallies, 1.0)[:, None, None]).reshape(voxel_count, model_width)
    places = jnp.transpose(coords, (2, 0, 1, 3)).reshape(3, voxel_count)
    stream = averaged + position_code(places, model_width)
    normed = normalize(stream)
    query = jnp.dot(normed, w_query, preferred_element_type=jnp.float32).astype(jnp.bfloat16)
    keys = jnp.dot(normed, w_key, preferred_element_type=jnp.float32).astype(jnp.bfloat16)
    values = jnp.dot(normed, w_value, preferred_element_type=jnp.float32).astype(jnp.bfloat16)
    half = BLOCK // 2

    def windowed(array):
        rolled = jnp.roll(array, -half, axis=0)
        return rolled.reshape(voxel_count // BLOCK, BLOCK, HEADS, HEAD_DIM).astype(jnp.float32)
    scores = jnp.einsum('wqhd,wkhd->whqk', windowed(query), windowed(keys)) / math.sqrt(HEAD_DIM)
    probs = jax.nn.softmax(scores, axis=-1).astype(jnp.bfloat16)
    probs = lax.optimization_barrier(probs).astype(jnp.float32)
    mixed = jnp.einsum('whqk,wkhd->wqhd', probs, windowed(values)).astype(jnp.bfloat16)
    mixed = jnp.roll(mixed.reshape(voxel_count, model_width), half, axis=0)
    attended = stream + jnp.dot(mixed, w_out, preferred_element_type=jnp.float32)
    normed_two = normalize(attended)
    hidden = jax.nn.gelu(jnp.dot(normed_two, w_up, preferred_element_type=jnp.float32), approximate=True).astype(jnp.bfloat16)
    encoded = attended + jnp.dot(hidden, w_down, preferred_element_type=jnp.float32)
    return encoded.astype(jnp.bfloat16).reshape(N_VIEW, N_SEG, ROWS_DEV, model_width)
```

```python
import functools
import math

import jax
import jax.numpy as jnp
from jax import lax
from jax.experimental import pallas as pl
from jax.experimental.pallas import tpu as pltpu
from jax.sharding import PartitionSpec as P

HEAD_DIM = 64
F32 = jnp.float32
BF16 = jnp.bfloat16
EXTRA = 8
VMEM_LIMIT = 60 * 1024 * 1024
VM = pl.BlockSpec(memory_space=pltpu.VMEM)
ANY = pl.BlockSpec(memory_space=pl.ANY)


def params(**kw):
    return pltpu.CompilerParams(vmem_limit_bytes=VMEM_LIMIT, **kw)


def dot(a, b):
    return lax.dot_general(a, b, (((1,), (0,)), ((), ())), preferred_element_type=F32)


def pack_kernel(patches, per_step, feat_ref, win_ref, idx_ref, extra_ref, out_ref, table):
    table_rows, width = table.shape
    full = (patches // 256) * 256

    @pl.when(pl.program_id(0) == 0)
    def _():
        table[full:, :] = jnp.zeros((table_rows - full, width), BF16)
        high = win_ref[...].astype(BF16)
        low = (win_ref[...] - high.astype(F32)).astype(BF16)
        for start in range(0, patches, 256):
            rows = feat_ref[start : min(start + 256, patches), :]
            table[start : start + rows.shape[0], :] = (dot(rows, high) + dot(rows, low)).astype(BF16)

    count = idx_ref.shape[0]
    picked = lax.broadcasted_iota(jnp.int32, (count, table_rows), 1) == idx_ref[...]
    rows = dot(picked.astype(F32).astype(BF16), table[...]).astype(BF16)
    each = count // per_step
    for i in range(per_step):
        out_ref[i, :each, :] = rows[i * each : (i + 1) * each, :]
        out_ref[i, each:, :] = extra_ref[i]


def pack(features, w_in, indices, extra):
    patches, channels = features.shape
    width = w_in.shape[1]
    segments = extra.shape[0]
    each = indices.shape[0] // segments
    per_step = 4
    table_rows = -(-patches // 128) * 128
    return pl.pallas_call(
        functools.partial(pack_kernel, patches, per_step),
        grid=(segments // per_step,),
        in_specs=[
            pl.BlockSpec((patches, channels), lambda i: (0, 0)),
            pl.BlockSpec((channels, width), lambda i: (0, 0)),
            pl.BlockSpec((per_step * each, 1), lambda i: (i, 0)),
            pl.BlockSpec((per_step, EXTRA, width), lambda i: (i, 0, 0)),
        ],
        out_specs=pl.BlockSpec((per_step, each + EXTRA, width), lambda i: (i, 0, 0)),
        out_shape=jax.ShapeDtypeStruct((segments, each + EXTRA, width), BF16),
        scratch_shapes=[pltpu.VMEM((table_rows, width), BF16)],
        compiler_params=params(),
        name="pack",
    )(features, w_in, indices, extra)


def gather_sums_kernel(slots_per, block, picks, place_ref, count_ref, recv_ref, *rest):
    outs, total = rest[:-1], rest[-1]
    total[...] = jnp.zeros_like(total)
    views = recv_ref.shape[0]
    width = recv_ref.shape[2]

    def add_view(j, carry):
        weights = recv_ref[j, slots_per * picks :, :].astype(F32)
        weights = jnp.concatenate(
            [weights[:, g * 128 : (g + 1) * 128] for g in range(picks // EXTRA)], axis=0
        ).astype(BF16)
        for c in range(slots_per):
            rows = recv_ref[j, c * picks : (c + 1) * picks, :]
            lifted = lax.dot_general(
                weights[:, c * block : (c + 1) * block],
                rows,
                (((0,), (0,)), ((), ())),
                preferred_element_type=F32,
            )
            start = pl.multiple_of(place_ref[j * slots_per + c], 8)
            total[pl.ds(start, block), :] += lifted
            mark = count_ref[j * slots_per + c]
            total[pl.ds(mark, 1), :] += jnp.ones((1, width), F32)
        return carry

    lax.fori_loop(0, views, add_view, 0)
    size = outs[0].shape[0]
    for i, out in enumerate(outs):
        out[...] = total[i * size : (i + 1) * size, :].astype(BF16)


def gather_sums(place, count, recv, slots_per, block, picks, half_blocks, parts):
    size = half_blocks * block + 8
    width = recv.shape[2]
    return pl.pallas_call(
        functools.partial(gather_sums_kernel, slots_per, block, picks),
        grid_spec=pltpu.PrefetchScalarGridSpec(
            num_scalar_prefetch=2,
            grid=(1,),
            in_specs=[pl.BlockSpec(recv.shape, lambda i, a, b: (0, 0, 0))],
            out_specs=[pl.BlockSpec((size, width), lambda i, a, b: (0, 0))] * parts,
            scratch_shapes=[pltpu.VMEM((parts * size + block + 8, width), F32)],
        ),
        out_shape=[jax.ShapeDtypeStruct((size, width), BF16)] * parts,
        compiler_params=params(dimension_semantics=("arbitrary",)),
        name="gather_sums",
    )(place, count, recv)


def normalize(values):
    average = jnp.mean(values, axis=-1, keepdims=True)
    centred = values - average
    spread = jnp.mean(centred * centred, axis=-1, keepdims=True)
    return (centred * lax.rsqrt(spread + 1e-05)).astype(BF16)


def project_kernel(block, half_blocks, *refs):
    sums = (refs[0:3], refs[3:6])
    pos_ref, wq_ref, wk_ref, wv_ref, stream_ref, q_ref, k_ref, v_ref = refs[6:]
    half_rows = half_blocks * block
    for h in range(2):
        base = h * half_rows

        def load(lo, hi):
            a, b, c = sums[h]
            return a[lo:hi, :].astype(F32) + b[lo:hi, :].astype(F32) + c[lo:hi, :].astype(F32)

        tally = jnp.maximum(load(half_rows, half_rows + 8), 1.0)
        for i in range(half_blocks):
            lo = i * block
            averaged = load(lo, lo + block) / tally[i : i + 1, :]
            stream_ref[base + lo : base + lo + block, :] = (
                averaged + pos_ref[base + lo : base + lo + block, :]
            )
        normed = normalize(stream_ref[base : base + half_rows, :])
        for w_ref, o_ref in ((wk_ref, k_ref), (wv_ref, v_ref), (wq_ref, q_ref)):
            o_ref[base : base + half_rows, :] = dot(normed, w_ref[...]).astype(BF16)


def project(sums, pos, w_query, w_key, w_value, block, half_blocks):
    rows, width = pos.shape
    return pl.pallas_call(
        functools.partial(project_kernel, block, half_blocks),
        in_specs=[VM] * 10,
        out_specs=[VM] * 4,
        out_shape=[jax.ShapeDtypeStruct((rows, width), F32)]
        + [jax.ShapeDtypeStruct((rows, width), BF16)] * 3,
        compiler_params=params(),
        name="project",
    )(*sums, pos, w_query, w_key, w_value)


def attend_kernel(
    block, stream_ref, q_ref, k_ref, v_ref, before_ref, after_ref, wout_ref, wup_hbm, wdown_hbm,
    out_ref, qx, kx, vx, mixed, attended, normed, total, wup, wdown, sems,
):
    rows, width = stream_ref.shape
    half = block // 2
    hidden_width = wup.shape[1]
    copies = [
        pltpu.make_async_copy(wup_hbm, wup, sems.at[0]),
        pltpu.make_async_copy(wdown_hbm, wdown, sems.at[1]),
    ]
    for c in copies:
        c.start()
    qx[:half, :] = jnp.zeros((half, width), BF16)
    qx[half : half + rows, :] = q_ref[...]
    qx[half + rows :, :] = jnp.zeros((half, width), BF16)
    for x, own, lane in ((kx, k_ref, 0), (vx, v_ref, width)):
        x[:half, :] = before_ref[:, lane : lane + width]
        x[half : half + rows, :] = own[...]
        x[half + rows :, :] = after_ref[:, lane : lane + width]
    low_lanes = lax.broadcasted_iota(jnp.int32, (block, 128), 1) < HEAD_DIM

    def window(w, carry):
        span = pl.ds(pl.multiple_of(w * block, block), block)
        for pair in range(width // 128):
            lanes = slice(pair * 128, (pair + 1) * 128)
            q, k, v = qx[span, lanes], kx[span, lanes], vx[span, lanes]
            zero = jnp.zeros_like(q)
            both = jnp.concatenate(
                [jnp.where(low_lanes, q, zero), jnp.where(low_lanes, zero, q)], axis=0
            )
            scores = lax.dot_general(
                both, k, (((1,), (1,)), ((), ())), preferred_element_type=F32
            ) * (1.0 / math.sqrt(HEAD_DIM))
            weights = jnp.exp(scores - jnp.max(scores, axis=-1, keepdims=True))
            probs = (weights / jnp.sum(weights, axis=-1, keepdims=True)).astype(BF16)
            out = dot(probs, v)
            mixed[span, lanes] = jnp.where(low_lanes, out[:block], out[block:]).astype(BF16)
        return carry

    lax.fori_loop(0, (rows + block) // block, window, 0)

    step = 256
    for start in range(0, rows, step):
        values = stream_ref[start : start + step, :] + dot(
            mixed[half + start : half + start + step, :], wout_ref[...]
        )
        attended[start : start + step, :] = values
        normed[start : start + step, :] = normalize(values)
    total[...] = attended[...]
    for c in copies:
        c.wait()
    chunk = 512

    def feed(i, carry):
        cols = pl.ds(pl.multiple_of(i * chunk, chunk), chunk)
        hidden = jax.nn.gelu(dot(normed[...], wup[:, cols]), approximate=True).astype(BF16)
        total[...] += dot(hidden, wdown[cols, :])
        return carry

    lax.fori_loop(0, hidden_width // chunk, feed, 0)
    out_ref[...] = total[...].astype(BF16)


def attend(stream, query, keys, values, before, after, w_out, w_up, w_down, block):
    rows, width = stream.shape
    hidden_width = w_up.shape[1]
    return pl.pallas_call(
        functools.partial(attend_kernel, block),
        in_specs=[VM] * 7 + [ANY] * 2,
        out_specs=VM,
        out_shape=jax.ShapeDtypeStruct((rows, width), BF16),
        scratch_shapes=[pltpu.VMEM((rows + block, width), BF16)] * 4
        + [
            pltpu.VMEM((rows, width), F32),
            pltpu.VMEM((rows, width), BF16),
            pltpu.VMEM((rows, width), F32),
            pltpu.VMEM((width, hidden_width), BF16),
            pltpu.VMEM((hidden_width, width), BF16),
            pltpu.SemaphoreType.DMA((2,)),
        ],
        compiler_params=params(),
        name="attend",
    )(stream, query, keys, values, before, after, w_out, w_up, w_down)


def position_code(places, model_width):
    freq_count = model_width // 6
    frequency = jnp.exp(-math.log(10000.0) * jnp.arange(freq_count, dtype=F32) / freq_count)
    columns = places.astype(F32).T
    pieces = []
    for a in range(3):
        angles = columns[:, a : a + 1] * frequency[None, :]
        pieces += [jnp.sin(angles), jnp.cos(angles)]
    return jnp.concatenate(pieces, axis=-1)


def shards(
    features, block_ids, patch_rows, lift_weights, coords, w_in,
    w_query, w_key, w_value, w_out, w_up, w_down,
):
    view_count, segments = lax.axis_size("view"), lax.axis_size("seg")
    rows_here = coords.shape[-1]
    _, _, slots, block, picks = lift_weights.shape
    width = w_in.shape[1]
    quarter = rows_here // block
    empty = view_count * quarter

    weights = jnp.transpose(lift_weights[0], (0, 3, 1, 2)).reshape(
        segments, picks // EXTRA, EXTRA, slots * block
    )
    weights = jnp.transpose(weights, (0, 2, 1, 3)).reshape(segments, EXTRA, -1)
    marks = jnp.broadcast_to(
        jnp.pad(block_ids[0].astype(BF16), ((0, 0), (0, 128 - slots)))[:, None, :],
        (segments, EXTRA, 128),
    )
    extra = jnp.concatenate([weights, marks], axis=-1)
    extra = jnp.pad(extra, ((0, 0), (0, 0), (0, width - extra.shape[-1])))
    payload = pack(features[0], w_in, patch_rows[0].reshape(-1, 1), extra)
    received = lax.all_to_all(payload, "seg", split_axis=0, concat_axis=0, tiled=True)

    pos = position_code(coords[0, 0], width)

    me = lax.axis_index("view")
    lane = slots * block * (picks // EXTRA)
    ids = received[:, slots * picks, lane : lane + slots].astype(jnp.int32).reshape(-1)
    half_blocks = quarter // 2
    size = half_blocks * block + 8
    parts = 2 * view_count
    within = ids % quarter
    part = ((ids // quarter - me) % view_count) * 2 + within // half_blocks
    place = jnp.where(
        ids == empty, parts * size, part * size + (within % half_blocks) * block
    ).astype(jnp.int32)
    count = jnp.where(
        ids == empty, parts * size + block, part * size + half_blocks * block + within % half_blocks
    ).astype(jnp.int32)
    own0, own1, up0, up1, far0, far1, down0, down1 = gather_sums(
        place, count, received, slots, block, picks, half_blocks, parts
    )
    up = [(i, (i + 1) % view_count) for i in range(view_count)]
    down = [(j, i) for i, j in up]

    def join(a, b):
        return (a.astype(F32) + b.astype(F32)).astype(BF16)

    far_up = lax.ppermute(far0, "view", up)
    far_down = lax.ppermute(far1, "view", down)
    near_up1 = lax.ppermute(up1, "view", up)
    near_down0 = lax.ppermute(down0, "view", down)
    near_up0 = lax.ppermute(join(up0, far_up), "view", up)
    near_down1 = lax.ppermute(join(down1, far_down), "view", down)

    stream, query, keys, values = project(
        (own0, near_down0, near_up0, own1, near_up1, near_down1),
        pos, w_query, w_key, w_value, block, half_blocks,
    )
    half = block // 2
    device_count = view_count * segments
    ring_up = [(i, (i + 1) % device_count) for i in range(device_count)]
    ring_down = [(j, i) for i, j in ring_up]
    last = jnp.concatenate([keys[rows_here - half :], values[rows_here - half :]], axis=1)
    first = jnp.concatenate([keys[:half], values[:half]], axis=1)
    before = lax.ppermute(last, ("view", "seg"), ring_up)
    after = lax.ppermute(first, ("view", "seg"), ring_down)
    encoded = attend(stream, query, keys, values, before, after, w_out, w_up, w_down, block)
    return encoded.reshape(1, 1, rows_here, width)


def solution(mesh):
    in_specs = (
        P(("view", "seg"), None, None),
        P(("view", "seg"), None, None),
        P(("view", "seg"), None, None, None),
        P(("view", "seg"), None, None, None, None),
        P("view", "seg", None, None),
        P(),
        P(),
        P(),
        P(),
        P(),
        P(),
        P(),
    )
    out_specs = P("view", "seg", None, None)
    return jax.shard_map(shards, mesh=mesh, in_specs=in_specs, out_specs=out_specs, check_vma=False)
```

```python
import functools
import math

import jax
import jax.numpy as jnp
from jax import lax
from jax.experimental import pallas as pl
from jax.experimental.pallas import tpu as pltpu
from jax.sharding import PartitionSpec as P


HEAD_DIM = 64
F32 = jnp.float32
BF16 = jnp.bfloat16
EXTRA = 16
VMEM_LIMIT = 60 * 1024 * 1024
VM = pl.BlockSpec(memory_space=pltpu.VMEM)
ANY = pl.BlockSpec(memory_space=pl.ANY)


def params(**kw):
    return pltpu.CompilerParams(vmem_limit_bytes=VMEM_LIMIT, **kw)


def dot(a, b):
    return lax.dot_general(a, b, (((1,), (0,)), ((), ())), preferred_element_type=F32)


def pack_kernel(patches, row_step, per_step, weighted, *refs):
    if weighted:
        ids_ref, feat_ref, win_ref, idx_ref, lift_ref, out_ref, table, places, high, low = refs
    else:
        feat_ref, win_ref, idx_ref, out_ref, table, places, high, low = refs
    table_rows, width = table.shape
    step = pl.program_id(0)
    row_steps = -(-patches // row_step)

    @pl.when(step == 0)
    def _():
        high[...] = win_ref[...].astype(BF16)
        low[...] = (win_ref[...] - high[...].astype(F32)).astype(BF16)
        turned = jnp.transpose(idx_ref[...].astype(F32)).astype(jnp.int32)
        for i in range(turned.shape[1]):
            places[i * 128 : (i + 1) * 128, :] = turned[:, i : i + 1]

    for s in range(row_steps):

        @pl.when(step == s)
        def _(s=s):
            start = s * row_step
            keep = min(row_step, table_rows - start)
            rows = feat_ref[:keep, :]
            values = (dot(rows, high[...]) + dot(rows, low[...])).astype(BF16)
            if start + keep > patches:
                live = lax.broadcasted_iota(jnp.int32, (keep, width), 0) < patches - start
                values = jnp.where(live, values, jnp.zeros_like(values))
            table[start : start + keep, :] = values

    @pl.when(step >= row_steps)
    def _():
        base = step - row_steps
        each = places.shape[0] // (per_step * (pl.num_programs(0) - row_steps))
        count = per_step * each
        spot = places[pl.ds(pl.multiple_of(base * count, count), count), :]
        picked = lax.broadcasted_iota(jnp.int32, (count, table_rows), 1) == spot
        rows = dot(picked.astype(F32).astype(BF16), table[...]).astype(BF16)
        for i in range(per_step):
            out_ref[i, :each, :] = rows[i * each : (i + 1) * each, :]
            if weighted:
                slots, _, block = lift_ref.shape[1:]
                both = jnp.concatenate([lift_ref[i, c].astype(F32) for c in range(slots)], axis=1)
                turned = jnp.transpose(both)
                for c in range(slots):
                    groups = [
                        turned[c * block + g * EXTRA : c * block + (g + 1) * EXTRA, :]
                        for g in range(block // EXTRA)
                    ]
                    out_ref[i, each:, c * 128 : (c + 1) * 128] = jnp.concatenate(
                        groups, axis=1
                    ).astype(BF16)
                lane = lax.broadcasted_iota(jnp.int32, (EXTRA, 128), 1)
                marks = jnp.zeros((EXTRA, 128), jnp.int32)
                for c in range(slots):
                    marks = jnp.where(lane == c, ids_ref[c, base * per_step + i], marks)
                out_ref[i, each:, slots * 128 : (slots + 1) * 128] = marks.astype(F32).astype(BF16)
                out_ref[i, each:, (slots + 1) * 128 :] = jnp.zeros(
                    (EXTRA, width - (slots + 1) * 128), BF16
                )


def pack(features, w_in, indices, segments, start, width, ids=None, lift=None):
    patches, channels = features.shape
    count = indices.shape[0] * indices.shape[1]
    each = count // segments
    per_step, row_step = 8, 512
    row_steps = -(-patches // row_step)
    table_rows = -(-patches // 128) * 128
    weighted = lift is not None

    def later(i):
        return jnp.maximum(i - row_steps, 0)

    in_specs = [
        pl.BlockSpec((row_step, channels), lambda i, *_: (jnp.minimum(i, row_steps - 1), 0)),
        pl.BlockSpec((channels, width), lambda i, *_: (0, start // width)),
        pl.BlockSpec(indices.shape, lambda i, *_: (0, 0)),
    ]
    operands = [features, w_in, indices]
    rows = each
    if weighted:
        in_specs.append(
            pl.BlockSpec((per_step,) + lift.shape[1:], lambda i, *_: (later(i), 0, 0, 0))
        )
        operands = [ids] + operands + [lift]
        rows += EXTRA
    return pl.pallas_call(
        functools.partial(pack_kernel, patches, row_step, per_step, weighted),
        grid_spec=pltpu.PrefetchScalarGridSpec(
            num_scalar_prefetch=int(weighted),
            grid=(row_steps + segments // per_step,),
            in_specs=in_specs,
            out_specs=pl.BlockSpec((per_step, rows, width), lambda i, *_: (later(i), 0, 0)),
            scratch_shapes=[
                pltpu.VMEM((table_rows, width), BF16),
                pltpu.VMEM((count, 1), jnp.int32),
                pltpu.VMEM((channels, width), BF16),
                pltpu.VMEM((channels, width), BF16),
            ],
        ),
        out_shape=jax.ShapeDtypeStruct((segments, rows, width), BF16),
        compiler_params=params(dimension_semantics=("arbitrary",)),
        name="pack",
    )(*operands)


def gather_sums_kernel(block, picks, half_blocks, counted, ids_ref, me_ref, rows_ref, weight_ref, *rest):
    outs, total = rest[-6:-1], rest[-1]
    total[...] = jnp.zeros_like(total)
    views, _, width = rows_ref.shape
    slots = ids_ref.shape[1]
    size = outs[2].shape[0]
    parts = 8
    depth = slots * picks * 4
    group = lax.broadcasted_iota(jnp.int32, (EXTRA, depth), 1) // picks
    me = me_ref[0]

    def add_view(j, carry):
        weights = weight_ref[j, :, :depth]
        zero = jnp.zeros_like(weights)
        left = jnp.concatenate([jnp.where(group == r, weights, zero) for r in range(slots * 4)], axis=0)
        rows = [rows_ref[j, c * picks : (c + 1) * picks, :] for c in range(slots)]
        right = jnp.concatenate([rows[c] for c in range(slots) for _ in range(4)], axis=0)
        lifted = dot(left, right)
        for c in range(slots):
            name = ids_ref[j, c]
            owner = name // (2 * half_blocks)
            within = name - owner * (2 * half_blocks)
            half = within // half_blocks
            within = within - half * half_blocks
            away = owner - me + jnp.where(owner < me, parts // 2, 0)
            start = (away * 2 + half) * size
            empty = name == parts * half_blocks
            place = jnp.where(empty, parts * size, start + within * block)
            place = pl.multiple_of(place, 8)
            total[pl.ds(place, block), :] += lifted[c * block : (c + 1) * block, :]
            if counted:
                mark = jnp.where(empty, parts * size + block, start + half_blocks * block + within)
                total[pl.ds(mark, 1), :] += jnp.ones((1, width), F32)
        return carry

    lax.fori_loop(0, views, add_view, 0, unroll=4)

    def part(away, half):
        first = (away * 2 + half) * size
        return total[first : first + size, :].astype(BF16)

    own, up_first, up_last, down_first, down_last = outs
    up_first[:size, :], up_first[size:, :] = part(1, 1), part(2, 0)
    down_first[:size, :], down_first[size:, :] = part(3, 0), part(2, 1)
    up_last[...], down_last[...] = part(1, 0), part(3, 1)
    own[:size, :], own[size:, :] = part(0, 0), part(0, 1)


def gather_sums(ids, me, rows, weights, block, picks, half_blocks, counted, *after):
    views, _, width = rows.shape
    count = ids.shape[1] * picks
    size = half_blocks * block + (8 if counted else 0)
    sizes = [2 * size, 2 * size, size, 2 * size, size]
    return pl.pallas_call(
        functools.partial(gather_sums_kernel, block, picks, half_blocks, counted),
        grid_spec=pltpu.PrefetchScalarGridSpec(
            num_scalar_prefetch=2,
            grid=(1,),
            in_specs=[
                pl.BlockSpec((views, count, width), lambda i, *_: (0, 0, 0)),
                pl.BlockSpec((views, EXTRA, weights.shape[2]), lambda i, *_: (0, count // EXTRA, 0)),
            ]
            + [ANY] * len(after),
            out_specs=[pl.BlockSpec((s, width), lambda i, *_: (0, 0)) for s in sizes],
            scratch_shapes=[pltpu.VMEM((8 * size + block + 8, width), F32)],
        ),
        out_shape=[jax.ShapeDtypeStruct((s, width), BF16) for s in sizes],
        compiler_params=params(dimension_semantics=("arbitrary",)),
        name="gather_sums",
    )(ids, me, rows, weights, *after)


def normalize(values):
    average = jnp.mean(values, axis=-1, keepdims=True)
    centred = values - average
    spread = jnp.mean(centred * centred, axis=-1, keepdims=True)
    return (centred * lax.rsqrt(spread + 1e-05)).astype(BF16)


def project_kernel(block, half_blocks, *refs):
    sums = (refs[0:5], refs[5:10])
    pos_ref, wq_ref, wk_ref, wv_ref, stream_ref, q_ref, k_ref, v_ref = refs[10:]
    half_rows = half_blocks * block
    for h in range(2):
        base = h * half_rows

        def load(column, lo, hi):
            own, below_first, above_first, below_last, above_last = sums[column]
            size = below_last.shape[0]
            first, last = (above_first, below_last) if h == 0 else (below_first, above_last)
            here = slice(h * size + lo, h * size + hi)
            return own[here, :].astype(F32) + first[lo:hi, :].astype(F32) + last[lo:hi, :].astype(F32)

        tally = jnp.maximum(load(0, half_rows, half_rows + 8), 1.0)
        for i in range(half_blocks):
            lo = i * block
            for column in range(2):
                start = sums[0][0].shape[1] * column
                lanes = slice(start, start + sums[column][0].shape[1])
                averaged = load(column, lo, lo + block) / tally[i : i + 1, : lanes.stop - lanes.start]
                stream_ref[base + lo : base + lo + block, lanes] = (
                    averaged + pos_ref[base + lo : base + lo + block, lanes]
                )
        normed = normalize(stream_ref[base : base + half_rows, :])
        for w_ref, o_ref in ((wk_ref, k_ref), (wv_ref, v_ref), (wq_ref, q_ref)):
            o_ref[base : base + half_rows, :] = dot(normed, w_ref[...]).astype(BF16)


def project(sums, pos, w_query, w_key, w_value, block, half_blocks):
    rows, width = pos.shape
    return pl.pallas_call(
        functools.partial(project_kernel, block, half_blocks),
        in_specs=[VM] * (len(sums) + 4),
        out_specs=[VM] * 4,
        out_shape=[jax.ShapeDtypeStruct((rows, width), F32)]
        + [jax.ShapeDtypeStruct((rows, width), BF16)] * 3,
        compiler_params=params(),
        name="project",
    )(*sums, pos, w_query, w_key, w_value)


def attend_kernel(
    block, stream_ref, q_ref, k_ref, v_ref, before_ref, after_ref, wout_ref, wup_hbm, wdown_hbm,
    out_ref, qx, kx, vx, mixed, attended, normed, total, wup, wdown, sems,
):
    rows, width = stream_ref.shape
    half = block // 2
    hidden_width = wup.shape[1]
    copies = [
        pltpu.make_async_copy(wup_hbm, wup, sems.at[0]),
        pltpu.make_async_copy(wdown_hbm, wdown, sems.at[1]),
    ]
    for c in copies:
        c.start()
    qx[:half, :] = jnp.zeros((half, width), BF16)
    qx[half : half + rows, :] = q_ref[...]
    qx[half + rows :, :] = jnp.zeros((half, width), BF16)
    for x, own, lane in ((kx, k_ref, 0), (vx, v_ref, width)):
        x[:half, :] = before_ref[:, lane : lane + width]
        x[half : half + rows, :] = own[...]
        x[half + rows :, :] = after_ref[:, lane : lane + width]
    low_lanes = lax.broadcasted_iota(jnp.int32, (block, 128), 1) < HEAD_DIM

    def window(w, carry):
        span = pl.ds(pl.multiple_of(w * block, block), block)
        for pair in range(width // 128):
            lanes = slice(pair * 128, (pair + 1) * 128)
            q, k, v = qx[span, lanes], kx[span, lanes], vx[span, lanes]
            zero = jnp.zeros_like(q)
            both = jnp.concatenate(
                [jnp.where(low_lanes, q, zero), jnp.where(low_lanes, zero, q)], axis=0
            )
            scores = lax.dot_general(
                both, k, (((1,), (1,)), ((), ())), preferred_element_type=F32
            ) * (1.0 / math.sqrt(HEAD_DIM))
            weights = jnp.exp(scores - jnp.max(scores, axis=-1, keepdims=True))
            probs = (weights / jnp.sum(weights, axis=-1, keepdims=True)).astype(BF16)
            out = dot(probs, v)
            mixed[span, lanes] = jnp.where(low_lanes, out[:block], out[block:]).astype(BF16)
        return carry

    lax.fori_loop(0, (rows + block) // block, window, 0)

    step = 256
    for start in range(0, rows, step):
        values = stream_ref[start : start + step, :] + dot(
            mixed[half + start : half + start + step, :], wout_ref[...]
        )
        attended[start : start + step, :] = values
        normed[start : start + step, :] = normalize(values)
    total[...] = attended[...]
    for c in copies:
        c.wait()
    chunk = 512

    def feed(i, carry):
        cols = pl.ds(pl.multiple_of(i * chunk, chunk), chunk)
        hidden = jax.nn.gelu(dot(normed[...], wup[:, cols]), approximate=True).astype(BF16)
        total[...] += dot(hidden, wdown[cols, :])
        return carry

    lax.fori_loop(0, hidden_width // chunk, feed, 0)
    out_ref[...] = total[...].astype(BF16)


def attend(stream, query, keys, values, before, after, w_out, w_up, w_down, block):
    rows, width = stream.shape
    hidden_width = w_up.shape[1]
    return pl.pallas_call(
        functools.partial(attend_kernel, block),
        in_specs=[VM] * 7 + [ANY] * 2,
        out_specs=VM,
        out_shape=jax.ShapeDtypeStruct((rows, width), BF16),
        scratch_shapes=[pltpu.VMEM((rows + block, width), BF16)] * 4
        + [
            pltpu.VMEM((rows, width), F32),
            pltpu.VMEM((rows, width), BF16),
            pltpu.VMEM((rows, width), F32),
            pltpu.VMEM((width, hidden_width), BF16),
            pltpu.VMEM((hidden_width, width), BF16),
            pltpu.SemaphoreType.DMA((2,)),
        ],
        compiler_params=params(),
        name="attend",
    )(stream, query, keys, values, before, after, w_out, w_up, w_down)


def position_kernel(coords_ref, freq_ref, out_ref):
    axes, rows = coords_ref.shape
    places = coords_ref[...].astype(F32)
    places = jnp.concatenate([places, jnp.zeros((8 - axes, rows), F32)], axis=0)
    columns = jnp.transpose(places)
    count = freq_ref.shape[1]
    for a in range(axes):
        angles = columns[:, a : a + 1] * freq_ref[...]
        out_ref[:, 2 * a * count : (2 * a + 1) * count] = jnp.sin(angles)
        out_ref[:, (2 * a + 1) * count : (2 * a + 2) * count] = jnp.cos(angles)


def position_code(places, model_width):
    freq_count = model_width // 6
    frequency = jnp.exp(-math.log(10000.0) * jnp.arange(freq_count, dtype=F32) / freq_count)
    return pl.pallas_call(
        position_kernel,
        in_specs=[VM] * 2,
        out_specs=VM,
        out_shape=jax.ShapeDtypeStruct((places.shape[1], model_width), F32),
        compiler_params=params(),
        name="position",
    )(places, frequency[None, :])


def share(parts, axis, count, half):
    own, up_first, up_last, down_first, down_last = parts
    up = [(i, (i + 1) % count) for i in range(count)]
    down = [(j, i) for i, j in up]

    def join(a, b):
        return (a.astype(F32) + b[half:].astype(F32)).astype(BF16)

    from_below = lax.ppermute(up_first, axis, up)
    from_above = lax.ppermute(down_first, axis, down)
    up_last, down_last = join(up_last, from_below), join(down_last, from_above)
    up_last, down_last = lax.ppermute(up_last, axis, up), lax.ppermute(down_last, axis, down)
    return [own, from_below, from_above, up_last, down_last]


def shards(
    features, block_ids, patch_rows, lift_weights, coords, w_in,
    w_query, w_key, w_value, w_out, w_up, w_down,
):
    view_count, segments = lax.axis_size("view"), lax.axis_size("seg")
    rows_here = coords.shape[-1]
    _, _, slots, block, picks = lift_weights.shape
    width = w_in.shape[1]
    quarter = rows_here // block
    half_blocks = quarter // 2

    indices = patch_rows[0].reshape(-1, 128)

    def send(payload):
        return lax.all_to_all(payload, "seg", split_axis=0, concat_axis=0, tiled=True)

    wide = width // 3 * 2
    by_row = jnp.transpose(lift_weights[0], (0, 1, 3, 2))
    first = send(pack(features[0], w_in, indices, segments, 0, wide, block_ids[0].T, by_row))
    second = send(pack(features[0], w_in, indices, segments, wide, width - wide))
    pos = position_code(coords[0, 0], width)
    me = lax.axis_index("view").astype(jnp.int32).reshape(1)
    ids = first[:, slots * picks, slots * 128 : slots * 128 + slots].astype(jnp.int32)

    def sums(rows, counted, *after):
        parts = gather_sums(ids, me, rows, first, block, picks, half_blocks, counted, *after)
        return share(parts, "view", view_count, parts[2].shape[0])

    shares = sums(first, True, pos)
    shares += sums(second, False)
    stream, query, keys, values = project(
        shares, pos, w_query, w_key, w_value, block, half_blocks
    )
    half = block // 2
    device_count = view_count * segments
    ring_up = [(i, (i + 1) % device_count) for i in range(device_count)]
    ring_down = [(j, i) for i, j in ring_up]
    last = jnp.concatenate([keys[rows_here - half :], values[rows_here - half :]], axis=1)
    first = jnp.concatenate([keys[:half], values[:half]], axis=1)
    before = lax.ppermute(last, ("view", "seg"), ring_up)
    after = lax.ppermute(first, ("view", "seg"), ring_down)
    encoded = attend(stream, query, keys, values, before, after, w_out, w_up, w_down, block)
    return encoded.reshape(1, 1, rows_here, width)


def solution(mesh):
    in_specs = (
        P(("view", "seg"), None, None),
        P(("view", "seg"), None, None),
        P(("view", "seg"), None, None, None),
        P(("view", "seg"), None, None, None, None),
        P("view", "seg", None, None),
        P(),
        P(),
        P(),
        P(),
        P(),
        P(),
        P(),
    )
    out_specs = P("view", "seg", None, None)

    return jax.shard_map(shards, mesh=mesh, in_specs=in_specs, out_specs=out_specs, check_vma=False)
```

```python
import functools
import math

import jax
import jax.numpy as jnp
from jax import lax
from jax.experimental import pallas as pl
from jax.experimental.pallas import tpu as pltpu
from jax.sharding import PartitionSpec as P


HEAD_DIM = 64
F32 = jnp.float32
BF16 = jnp.bfloat16
EXTRA = 16
VM = pl.BlockSpec(memory_space=pltpu.VMEM)
ANY = pl.BlockSpec(memory_space=pl.ANY)


def params(megabytes, **kw):
    return pltpu.CompilerParams(vmem_limit_bytes=megabytes * 1024 * 1024, **kw)


def dot(a, b):
    return lax.dot_general(a, b, (((1,), (0,)), ((), ())), preferred_element_type=F32)


def pack_kernel(start, per_step, weighted, *refs):
    if weighted:
        ids_ref, feat_hbm, win_hbm, idx_ref, lift_ref, out_hbm = refs[:6]
    else:
        feat_hbm, win_hbm, idx_ref, out_hbm = refs[:4]
    feat, win, table, places, packed, feat_sems, win_sem, out_sems = refs[-8:]
    patches = feat.shape[0]
    table_rows, width = table.shape
    segments = packed.shape[0]
    count = per_step * (places.shape[0] // segments)
    each = count // per_step
    row_step = 256

    win_copy = pltpu.make_async_copy(win_hbm.at[:, start : start + width], win, win_sem)
    win_copy.start()
    spans = [slice(s, min(s + row_step, patches)) for s in range(0, patches, row_step)]
    feat_copies = [
        pltpu.make_async_copy(feat_hbm.at[span, :], feat.at[span, :], feat_sems.at[i])
        for i, span in enumerate(spans)
    ]
    for copy in feat_copies:
        copy.start()
    turned = jnp.transpose(idx_ref[...].astype(F32)).astype(jnp.int32)
    for i in range(turned.shape[1]):
        places[i * 128 : (i + 1) * 128, :] = turned[:, i : i + 1]
    table[spans[-1].start :, :] = jnp.zeros((table_rows - spans[-1].start, width), BF16)
    win_copy.wait()
    weights = win[...].astype(BF16)
    for copy, span in zip(feat_copies, spans):
        copy.wait()
        table[span, :] = dot(feat[span, :], weights).astype(BF16)

    def out_copy(base):
        own = pl.ds(base * per_step, per_step)
        return pltpu.make_async_copy(packed.at[own], out_hbm.at[own], out_sems.at[base])

    def pick(base, carry):
        spot = places[pl.ds(pl.multiple_of(base * count, count), count), :]
        picked = lax.broadcasted_iota(jnp.int32, (count, table_rows), 1) == spot
        rows = dot(picked.astype(F32).astype(BF16), table[...]).astype(BF16)
        for i in range(per_step):
            segment = base * per_step + i
            packed[segment, :each, :] = rows[i * each : (i + 1) * each, :]
            if weighted:
                slots, _, block = lift_ref.shape[1:]
                both = jnp.concatenate(
                    [lift_ref[segment, c].astype(F32) for c in range(slots)], axis=1
                )
                turned = jnp.transpose(both)
                for c in range(slots):
                    groups = [
                        turned[c * block + g * EXTRA : c * block + (g + 1) * EXTRA, :]
                        for g in range(block // EXTRA)
                    ]
                    packed[segment, each:, c * 128 : (c + 1) * 128] = jnp.concatenate(
                        groups, axis=1
                    ).astype(BF16)
                lane = lax.broadcasted_iota(jnp.int32, (EXTRA, 128), 1)
                marks = jnp.zeros((EXTRA, 128), jnp.int32)
                for c in range(slots):
                    marks = jnp.where(lane == c, ids_ref[c, segment], marks)
                packed[segment, each:, slots * 128 : (slots + 1) * 128] = marks.astype(F32).astype(BF16)
                packed[segment, each:, (slots + 1) * 128 :] = jnp.zeros(
                    (EXTRA, width - (slots + 1) * 128), BF16
                )
        out_copy(base).start()
        return carry

    steps = segments // per_step
    lax.fori_loop(0, steps, pick, 0)
    for base in range(steps):
        out_copy(base).wait()


def pack(features, w_in, indices, segments, start, width, ids=None, lift=None):
    patches, channels = features.shape
    count = indices.shape[0] * indices.shape[1]
    per_step = 8
    weighted = lift is not None
    rows = count // segments + (EXTRA if weighted else 0)
    operands, in_specs = [features, w_in, indices], [ANY, ANY, VM]
    if weighted:
        operands = [ids] + operands + [lift]
        in_specs = [pl.BlockSpec(memory_space=pltpu.SMEM)] + in_specs + [VM]
    return pl.pallas_call(
        functools.partial(pack_kernel, start, per_step, weighted),
        in_specs=in_specs,
        out_specs=ANY,
        scratch_shapes=[
            pltpu.VMEM((patches, channels), BF16),
            pltpu.VMEM((channels, width), F32),
            pltpu.VMEM((-(-patches // 128) * 128, width), BF16),
            pltpu.VMEM((count, 1), jnp.int32),
            pltpu.VMEM((segments, rows, width), BF16),
            pltpu.SemaphoreType.DMA((-(-patches // 256),)),
            pltpu.SemaphoreType.DMA(()),
            pltpu.SemaphoreType.DMA((segments // per_step,)),
        ],
        out_shape=jax.ShapeDtypeStruct((segments, rows, width), BF16),
        compiler_params=params(60),
        name="pack",
    )(*operands)


def gather_sums_kernel(block, picks, half_blocks, counted, ids_ref, me_ref, rows_ref, weight_ref, *rest):
    outs, total = rest[-6:-1], rest[-1]
    step = pl.program_id(0)
    views, _, width = rows_ref.shape

    @pl.when(step == 0)
    def _():
        total[...] = jnp.zeros_like(total)

    slots = ids_ref.shape[1]
    size = outs[2].shape[0]
    parts = 8
    depth = slots * picks * 4
    group = lax.broadcasted_iota(jnp.int32, (EXTRA, depth), 1) // picks
    me = me_ref[0]

    def add_view(j, carry):
        weights = weight_ref[j, :, :depth]
        zero = jnp.zeros_like(weights)
        left = jnp.concatenate([jnp.where(group == r, weights, zero) for r in range(slots * 4)], axis=0)
        rows = [rows_ref[j, c * picks : (c + 1) * picks, :] for c in range(slots)]
        right = jnp.concatenate([rows[c] for c in range(slots) for _ in range(4)], axis=0)
        lifted = dot(left, right)
        for c in range(slots):
            name = ids_ref[step * views + j, c]
            owner = name // (2 * half_blocks)
            within = name - owner * (2 * half_blocks)
            half = within // half_blocks
            within = within - half * half_blocks
            away = owner - me + jnp.where(owner < me, parts // 2, 0)
            start = (away * 2 + half) * size
            empty = name == parts * half_blocks
            place = jnp.where(empty, parts * size, start + within * block)
            place = pl.multiple_of(place, 8)
            total[pl.ds(place, block), :] += lifted[c * block : (c + 1) * block, :]
            if counted:
                mark = jnp.where(empty, parts * size + block, start + half_blocks * block + within)
                total[pl.ds(mark, 1), :] += jnp.ones((1, width), F32)
        return carry

    lax.fori_loop(0, views, add_view, 0, unroll=4)

    @pl.when(step == pl.num_programs(0) - 1)
    def _():
        def part(away, half):
            first = (away * 2 + half) * size
            return total[first : first + size, :].astype(BF16)

        own, up_first, up_last, down_first, down_last = outs
        up_first[:size, :], up_first[size:, :] = part(1, 1), part(2, 0)
        down_first[:size, :], down_first[size:, :] = part(3, 0), part(2, 1)
        up_last[...], down_last[...] = part(1, 0), part(3, 1)
        own[:size, :], own[size:, :] = part(0, 0), part(0, 1)


def gather_sums(ids, me, rows, weights, block, picks, half_blocks, counted, *after):
    views, _, width = rows.shape
    count = ids.shape[1] * picks
    size = half_blocks * block + (8 if counted else 0)
    sizes = [2 * size, 2 * size, size, 2 * size, size]
    return pl.pallas_call(
        functools.partial(gather_sums_kernel, block, picks, half_blocks, counted),
        grid_spec=pltpu.PrefetchScalarGridSpec(
            num_scalar_prefetch=2,
            grid=(views // 8,),
            in_specs=[
                pl.BlockSpec((8, count, width), lambda i, *_: (i, 0, 0)),
                pl.BlockSpec((8, EXTRA, weights.shape[2]), lambda i, *_: (i, count // EXTRA, 0)),
            ]
            + [ANY] * len(after),
            out_specs=[pl.BlockSpec((s, width), lambda i, *_: (0, 0)) for s in sizes],
            scratch_shapes=[pltpu.VMEM((8 * size + block + 8, width), F32)],
        ),
        out_shape=[jax.ShapeDtypeStruct((s, width), BF16) for s in sizes],
        compiler_params=params(24, dimension_semantics=("arbitrary",)),
        name="gather_sums",
    )(ids, me, rows, weights, *after)


def normalize(values):
    average = jnp.mean(values, axis=-1, keepdims=True)
    centred = values - average
    spread = jnp.mean(centred * centred, axis=-1, keepdims=True)
    return (centred * lax.rsqrt(spread + 1e-05)).astype(BF16)


def project_kernel(block, half_blocks, *refs):
    sums = (refs[0:5], refs[5:10])
    pos_ref, wq_ref, wk_ref, wv_ref, stream_ref, q_ref, k_ref, v_ref = refs[10:]
    half_rows = half_blocks * block
    for h in range(2):
        base = h * half_rows

        def load(column, lo, hi):
            own, below_first, above_first, below_last, above_last = sums[column]
            size = below_last.shape[0]
            first, last = (above_first, below_last) if h == 0 else (below_first, above_last)
            here = slice(h * size + lo, h * size + hi)
            return own[here, :].astype(F32) + first[lo:hi, :].astype(F32) + last[lo:hi, :].astype(F32)

        tally = jnp.maximum(load(0, half_rows, half_rows + 8), 1.0)
        for i in range(half_blocks):
            lo = i * block
            for column in range(2):
                start = sums[0][0].shape[1] * column
                lanes = slice(start, start + sums[column][0].shape[1])
                averaged = load(column, lo, lo + block) / tally[i : i + 1, : lanes.stop - lanes.start]
                stream_ref[base + lo : base + lo + block, lanes] = (
                    averaged + pos_ref[base + lo : base + lo + block, lanes]
                )
        normed = normalize(stream_ref[base : base + half_rows, :])
        for w_ref, o_ref in ((wk_ref, k_ref), (wv_ref, v_ref), (wq_ref, q_ref)):
            o_ref[base : base + half_rows, :] = dot(normed, w_ref[...]).astype(BF16)


def project(sums, pos, w_query, w_key, w_value, block, half_blocks):
    rows, width = pos.shape
    return pl.pallas_call(
        functools.partial(project_kernel, block, half_blocks),
        in_specs=[VM] * (len(sums) + 4),
        out_specs=[VM] * 4,
        out_shape=[jax.ShapeDtypeStruct((rows, width), F32)]
        + [jax.ShapeDtypeStruct((rows, width), BF16)] * 3,
        compiler_params=params(24),
        name="project",
    )(*sums, pos, w_query, w_key, w_value)


def attend_kernel(
    block, stream_ref, q_ref, k_ref, v_ref, before_ref, after_ref, wout_ref, wup, wdown,
    out_ref, qx, kx, vx, mixed, normed, total,
):
    rows, width = stream_ref.shape
    half = block // 2
    hidden_width = wup.shape[1]
    qx[:half, :] = jnp.zeros((half, width), BF16)
    qx[half : half + rows, :] = q_ref[...]
    qx[half + rows :, :] = jnp.zeros((half, width), BF16)
    for x, own, lane in ((kx, k_ref, 0), (vx, v_ref, width)):
        x[:half, :] = before_ref[:, lane : lane + width]
        x[half : half + rows, :] = own[...]
        x[half + rows :, :] = after_ref[:, lane : lane + width]
    low_lanes = lax.broadcasted_iota(jnp.int32, (block, 128), 1) < HEAD_DIM

    def window(w, carry):
        span = pl.ds(pl.multiple_of(w * block, block), block)
        for pair in range(width // 128):
            lanes = slice(pair * 128, (pair + 1) * 128)
            q, k, v = qx[span, lanes], kx[span, lanes], vx[span, lanes]
            zero = jnp.zeros_like(q)
            both = jnp.concatenate(
                [jnp.where(low_lanes, q, zero), jnp.where(low_lanes, zero, q)], axis=0
            )
            scores = lax.dot_general(
                both, k, (((1,), (1,)), ((), ())), preferred_element_type=F32
            ) * (1.0 / math.sqrt(HEAD_DIM))
            weights = jnp.exp(scores - jnp.max(scores, axis=-1, keepdims=True))
            probs = (weights / jnp.sum(weights, axis=-1, keepdims=True)).astype(BF16)
            out = dot(probs, v)
            mixed[span, lanes] = jnp.where(low_lanes, out[:block], out[block:]).astype(BF16)
        return carry

    lax.fori_loop(0, (rows + block) // block, window, 0, unroll=3)

    step = 256
    for start in range(0, rows, step):
        values = stream_ref[start : start + step, :] + dot(
            mixed[half + start : half + start + step, :], wout_ref[...]
        )
        total[start : start + step, :] = values
        normed[start : start + step, :] = normalize(values)
    chunk = 768
    for i in range(hidden_width // chunk):
        cols = slice(i * chunk, (i + 1) * chunk)
        hidden = jax.nn.gelu(dot(normed[...], wup[:, cols]), approximate=True).astype(BF16)
        total[...] += dot(hidden, wdown[cols, :])
    out_ref[...] = total[...].astype(BF16)


def attend(stream, query, keys, values, before, after, w_out, w_up, w_down, block):
    rows, width = stream.shape
    return pl.pallas_call(
        functools.partial(attend_kernel, block),
        in_specs=[VM] * 9,
        out_specs=VM,
        out_shape=jax.ShapeDtypeStruct((rows, width), BF16),
        scratch_shapes=[pltpu.VMEM((rows + block, width), BF16)] * 4
        + [
            pltpu.VMEM((rows, width), BF16),
            pltpu.VMEM((rows, width), F32),
        ],
        compiler_params=params(30),
        name="attend",
    )(stream, query, keys, values, before, after, w_out, w_up, w_down)


def position_kernel(coords_ref, freq_ref, out_ref):
    axes, rows = coords_ref.shape
    places = coords_ref[...].astype(F32)
    places = jnp.concatenate([places, jnp.zeros((8 - axes, rows), F32)], axis=0)
    columns = jnp.transpose(places)
    count = freq_ref.shape[1]
    for a in range(axes):
        angles = columns[:, a : a + 1] * freq_ref[...]
        out_ref[:, 2 * a * count : (2 * a + 1) * count] = jnp.sin(angles)
        out_ref[:, (2 * a + 1) * count : (2 * a + 2) * count] = jnp.cos(angles)


def position_code(places, model_width):
    freq_count = model_width // 6
    frequency = jnp.exp(-math.log(10000.0) * jnp.arange(freq_count, dtype=F32) / freq_count)
    return pl.pallas_call(
        position_kernel,
        in_specs=[VM] * 2,
        out_specs=VM,
        out_shape=jax.ShapeDtypeStruct((places.shape[1], model_width), F32),
        compiler_params=params(16),
        name="position",
    )(places, frequency[None, :])


def share(parts, axis, count, half):
    own, up_first, up_last, down_first, down_last = parts
    up = [(i, (i + 1) % count) for i in range(count)]
    down = [(j, i) for i, j in up]

    def join(a, b):
        return (a.astype(F32) + b[half:].astype(F32)).astype(BF16)

    from_below = lax.ppermute(up_first, axis, up)
    from_above = lax.ppermute(down_first, axis, down)
    up_last, down_last = join(up_last, from_below), join(down_last, from_above)
    up_last, down_last = lax.ppermute(up_last, axis, up), lax.ppermute(down_last, axis, down)
    return [own, from_below, from_above, up_last, down_last]


def shards(
    features, block_ids, patch_rows, lift_weights, coords, w_in,
    w_query, w_key, w_value, w_out, w_up, w_down,
):
    view_count, segments = lax.axis_size("view"), lax.axis_size("seg")
    rows_here = coords.shape[-1]
    _, _, slots, block, picks = lift_weights.shape
    width = w_in.shape[1]
    quarter = rows_here // block
    half_blocks = quarter // 2

    indices = patch_rows[0].reshape(-1, 128)

    def send(payload):
        return lax.all_to_all(payload, "seg", split_axis=0, concat_axis=0, tiled=True)

    wide = width // 3 * 2
    by_row = jnp.transpose(lift_weights[0], (0, 1, 3, 2))
    first = send(pack(features[0], w_in, indices, segments, 0, wide, block_ids[0].T, by_row))
    second = send(pack(features[0], w_in, indices, segments, wide, width - wide))
    pos = position_code(coords[0, 0], width)
    me = lax.axis_index("view").astype(jnp.int32).reshape(1)
    ids = first[:, slots * picks, slots * 128 : slots * 128 + slots].astype(jnp.int32)

    def sums(rows, counted, *after):
        parts = gather_sums(ids, me, rows, first, block, picks, half_blocks, counted, *after)
        return share(parts, "view", view_count, parts[2].shape[0])

    shares = sums(first, True, pos)
    shares += sums(second, False)
    stream, query, keys, values = project(
        shares, pos, w_query, w_key, w_value, block, half_blocks
    )
    half = block // 2
    device_count = view_count * segments
    ring_up = [(i, (i + 1) % device_count) for i in range(device_count)]
    ring_down = [(j, i) for i, j in ring_up]
    last = jnp.concatenate([keys[rows_here - half :], values[rows_here - half :]], axis=1)
    first = jnp.concatenate([keys[:half], values[:half]], axis=1)
    before = lax.ppermute(last, ("view", "seg"), ring_up)
    after = lax.ppermute(first, ("view", "seg"), ring_down)
    encoded = attend(stream, query, keys, values, before, after, w_out, w_up, w_down, block)
    return encoded.reshape(1, 1, rows_here, width)


def solution(mesh):
    in_specs = (
        P(("view", "seg"), None, None),
        P(("view", "seg"), None, None),
        P(("view", "seg"), None, None, None),
        P(("view", "seg"), None, None, None, None),
        P("view", "seg", None, None),
        P(),
        P(),
        P(),
        P(),
        P(),
        P(),
        P(),
    )
    out_specs = P("view", "seg", None, None)

    return jax.shard_map(shards, mesh=mesh, in_specs=in_specs, out_specs=out_specs, check_vma=False)
```

```python
import functools
import math

import jax
import jax.numpy as jnp
from jax import lax
from jax.experimental import pallas as pl
from jax.experimental.pallas import tpu as pltpu
from jax.sharding import PartitionSpec as P


HEAD_DIM = 64
F32 = jnp.float32
BF16 = jnp.bfloat16
EXTRA = 16
VM = pl.BlockSpec(memory_space=pltpu.VMEM)
ANY = pl.BlockSpec(memory_space=pl.ANY)


def params(megabytes, **kw):
    return pltpu.CompilerParams(vmem_limit_bytes=megabytes * 1024 * 1024, **kw)


def dot(a, b):
    return lax.dot_general(a, b, (((1,), (0,)), ((), ())), preferred_element_type=F32)


def pack_kernel(start, per_step, weighted, *refs):
    if weighted:
        ids_ref, feat_hbm, win_hbm, idx_ref, lift_ref, out_hbm = refs[:6]
    else:
        feat_hbm, win_hbm, idx_ref, out_hbm = refs[:4]
    feat, win, table, places, packed, feat_sems, win_sem, out_sems = refs[-8:]
    patches = feat.shape[0]
    table_rows, width = table.shape
    segments = packed.shape[0]
    count = per_step * (places.shape[0] // segments)
    each = count // per_step
    row_step = 512

    win_copy = pltpu.make_async_copy(win_hbm.at[:, start : start + width], win, win_sem)
    spans = [slice(s, min(s + row_step, patches)) for s in range(0, patches, row_step)]
    feat_copies = [
        pltpu.make_async_copy(feat_hbm.at[span, :], feat.at[span, :], feat_sems.at[i])
        for i, span in enumerate(spans)
    ]
    win_copy.start()
    for copy in feat_copies:
        copy.start()
    turned = jnp.transpose(idx_ref[...].astype(F32)).astype(jnp.int32)
    for i in range(turned.shape[1]):
        places[i * 128 : (i + 1) * 128, :] = turned[:, i : i + 1]
    table[spans[-1].start :, :] = jnp.zeros((table_rows - spans[-1].start, width), BF16)

    if weighted:
        slots, depth, block = lift_ref.shape[1:]
        line = slots * block
        lane = lax.broadcasted_iota(jnp.int32, (depth, line), 1) // EXTRA
        pickers = lax.broadcasted_iota(jnp.int32, (EXTRA, line), 1) % EXTRA
        pickers = (pickers == lax.broadcasted_iota(jnp.int32, (EXTRA, line), 0)).astype(F32).astype(BF16)
        mark_lane = lax.broadcasted_iota(jnp.int32, (EXTRA, width - 2 * line), 1)

        def weigh(segment, carry):
            both = jnp.concatenate([lift_ref[segment, c] for c in range(slots)], axis=1)
            zero = jnp.zeros_like(both)
            apart = jnp.concatenate(
                [jnp.where(lane == g, both, zero) for g in range(line // EXTRA)], axis=0
            )
            packed[segment, each:, : 2 * line] = lax.dot_general(
                pickers, apart, (((1,), (1,)), ((), ())), preferred_element_type=F32
            ).astype(BF16)
            marks = jnp.zeros(mark_lane.shape, jnp.int32)
            for c in range(slots):
                marks = jnp.where(mark_lane == c, ids_ref[c, segment], marks)
            packed[segment, each:, 2 * line :] = marks.astype(F32).astype(BF16)
            return carry

        lax.fori_loop(0, segments, weigh, 0, unroll=8)

    win_copy.wait()
    weights = win[...].astype(BF16)
    for copy, span in zip(feat_copies, spans):
        copy.wait()
        table[span, :] = dot(feat[span, :], weights).astype(BF16)

    def out_copy(base):
        own = pl.ds(base * per_step, per_step)
        return pltpu.make_async_copy(packed.at[own], out_hbm.at[own], out_sems.at[base])

    def pick(base, carry):
        spot = places[pl.ds(pl.multiple_of(base * count, count), count), :]
        picked = lax.broadcasted_iota(jnp.int32, (count, table_rows), 1) == spot
        rows = dot(picked.astype(F32).astype(BF16), table[...]).astype(BF16)
        for i in range(per_step):
            packed[base * per_step + i, :each, :] = rows[i * each : (i + 1) * each, :]
        out_copy(base).start()
        return carry

    steps = segments // per_step
    lax.fori_loop(0, steps, pick, 0, unroll=True)
    for base in range(steps):
        out_copy(base).wait()


def pack(features, w_in, indices, segments, start, width, ids=None, lift=None):
    patches, channels = features.shape
    count = indices.shape[0] * indices.shape[1]
    per_step = 8
    weighted = lift is not None
    rows = count // segments + (EXTRA if weighted else 0)
    operands, in_specs = [features, w_in, indices], [ANY, ANY, VM]
    if weighted:
        operands = [ids] + operands + [lift]
        in_specs = [pl.BlockSpec(memory_space=pltpu.SMEM)] + in_specs + [VM]
    return pl.pallas_call(
        functools.partial(pack_kernel, start, per_step, weighted),
        in_specs=in_specs,
        out_specs=ANY,
        scratch_shapes=[
            pltpu.VMEM((patches, channels), BF16),
            pltpu.VMEM((channels, width), F32),
            pltpu.VMEM((-(-patches // 128) * 128, width), BF16),
            pltpu.VMEM((count, 1), jnp.int32),
            pltpu.VMEM((segments, rows, width), BF16),
            pltpu.SemaphoreType.DMA((-(-patches // 512),)),
            pltpu.SemaphoreType.DMA(()),
            pltpu.SemaphoreType.DMA((segments // per_step,)),
        ],
        out_shape=jax.ShapeDtypeStruct((segments, rows, width), BF16),
        compiler_params=params(60),
        name="pack",
    )(*operands)


def gather_sums_kernel(block, picks, half_blocks, counted, ids_ref, me_ref, rows_ref, weight_ref, *rest):
    outs, total, stage, sems = rest[-8:-3], rest[-3], rest[-2], rest[-1]
    step = pl.program_id(0)
    views, _, width = rows_ref.shape

    @pl.when(step == 0)
    def _():
        total[...] = jnp.zeros_like(total)

    slots = ids_ref.shape[1]
    size = outs[2].shape[0]
    parts = 8
    depth = slots * picks * 4
    group = lax.broadcasted_iota(jnp.int32, (EXTRA, depth), 1) // picks
    me = me_ref[0]

    def add_view(j, carry):
        weights = weight_ref[j, :, :depth]
        zero = jnp.zeros_like(weights)
        left = jnp.concatenate([jnp.where(group == r, weights, zero) for r in range(slots * 4)], axis=0)
        rows = [rows_ref[j, c * picks : (c + 1) * picks, :] for c in range(slots)]
        right = jnp.concatenate([rows[c] for c in range(slots) for _ in range(4)], axis=0)
        lifted = dot(left, right)
        for c in range(slots):
            name = ids_ref[step * views + j, c]
            owner = name // (2 * half_blocks)
            within = name - owner * (2 * half_blocks)
            half = within // half_blocks
            within = within - half * half_blocks
            away = owner - me + jnp.where(owner < me, parts // 2, 0)
            start = (away * 2 + half) * size
            empty = name == parts * half_blocks
            place = jnp.where(empty, parts * size, start + within * block)
            place = pl.multiple_of(place, 8)
            total[pl.ds(place, block), :] += lifted[c * block : (c + 1) * block, :]
            if counted:
                mark = jnp.where(empty, parts * size + block, start + half_blocks * block + within)
                total[pl.ds(mark, 1), :] += jnp.ones((1, width), F32)
        return carry

    lax.fori_loop(0, views, add_view, 0, unroll=4)

    @pl.when(step == pl.num_programs(0) - 1)
    def _():
        own, up_first, up_last, down_first, down_last = outs
        order = (
            (up_first, 0, 1, 1), (up_first, 1, 2, 0), (down_first, 0, 3, 0), (down_first, 1, 2, 1),
            (up_last, 0, 1, 0), (down_last, 0, 3, 1), (own, 0, 0, 0), (own, 1, 0, 1),
        )
        copies = []
        for i, (out, place, away, half) in enumerate(order):
            first = (away * 2 + half) * size
            stage[i] = total[first : first + size, :].astype(BF16)
            copies.append(
                pltpu.make_async_copy(
                    stage.at[i], out.at[place * size : (place + 1) * size, :], sems.at[i]
                )
            )
            copies[-1].start()
        for copy in copies:
            copy.wait()


def gather_sums(ids, me, rows, weights, block, picks, half_blocks, counted):
    views, _, width = rows.shape
    count = ids.shape[1] * picks
    size = half_blocks * block + (8 if counted else 0)
    sizes = [2 * size, 2 * size, size, 2 * size, size]
    return pl.pallas_call(
        functools.partial(gather_sums_kernel, block, picks, half_blocks, counted),
        grid_spec=pltpu.PrefetchScalarGridSpec(
            num_scalar_prefetch=2,
            grid=(views // 8,),
            in_specs=[
                pl.BlockSpec((8, count, width), lambda i, *_: (i, 0, 0)),
                pl.BlockSpec((8, EXTRA, weights.shape[2]), lambda i, *_: (i, count // EXTRA, 0)),
            ],
            out_specs=[pl.BlockSpec(memory_space=pltpu.HBM)] * len(sizes),
            scratch_shapes=[
                pltpu.VMEM((8 * size + block + 8, width), F32),
                pltpu.VMEM((8, size, width), BF16),
                pltpu.SemaphoreType.DMA((8,)),
            ],
        ),
        out_shape=[
            (pltpu.HBM if counted and i in (0, 2, 4) else jax.ShapeDtypeStruct)((s, width), BF16)
            for i, s in enumerate(sizes)
        ],
        compiler_params=params(20, dimension_semantics=("arbitrary",)),
        name="gather_sums",
    )(ids, me, rows, weights)


def normalize(values):
    average = jnp.mean(values, axis=-1, keepdims=True)
    centred = values - average
    spread = jnp.mean(centred * centred, axis=-1, keepdims=True)
    return (centred * lax.rsqrt(spread + 1e-05)).astype(BF16)


def project_kernel(block, half_blocks, *refs):
    sums = (refs[0:5], refs[5:10])
    pos_ref, wq_ref, wk_ref, wv_ref, stream_ref, q_ref, k_ref, v_ref = refs[10:]
    half_rows = half_blocks * block
    for h in range(2):
        base = h * half_rows

        def load(column, lo, hi):
            own, below_first, above_first, below_last, above_last = sums[column]
            size = below_last.shape[0]
            first, last = (above_first, below_last) if h == 0 else (below_first, above_last)
            here = slice(h * size + lo, h * size + hi)
            return own[here, :].astype(F32) + first[lo:hi, :].astype(F32) + last[lo:hi, :].astype(F32)

        tally = jnp.maximum(load(0, half_rows, half_rows + 8), 1.0)
        for i in range(half_blocks):
            lo = i * block
            for column in range(2):
                start = sums[0][0].shape[1] * column
                lanes = slice(start, start + sums[column][0].shape[1])
                averaged = load(column, lo, lo + block) / tally[i : i + 1, : lanes.stop - lanes.start]
                stream_ref[base + lo : base + lo + block, lanes] = (
                    averaged + pos_ref[base + lo : base + lo + block, lanes]
                )
        normed = normalize(stream_ref[base : base + half_rows, :])
        for w_ref, o_ref in ((wk_ref, k_ref), (wv_ref, v_ref), (wq_ref, q_ref)):
            o_ref[base : base + half_rows, :] = dot(normed, w_ref[...]).astype(BF16)


def project(sums, pos, w_query, w_key, w_value, block, half_blocks):
    rows, width = pos.shape
    return pl.pallas_call(
        functools.partial(project_kernel, block, half_blocks),
        in_specs=[VM] * (len(sums) + 4),
        out_specs=[VM] * 4,
        out_shape=[jax.ShapeDtypeStruct((rows, width), F32)]
        + [jax.ShapeDtypeStruct((rows, width), BF16)] * 3,
        compiler_params=params(16),
        cost_estimate=pl.CostEstimate(flops=6 * rows * width * width, bytes_accessed=12 * rows * width, transcendentals=0),
        name="project",
    )(*sums, pos, w_query, w_key, w_value)


def attend_kernel(
    block, stream_ref, q_ref, k_ref, v_ref, before_ref, after_ref, wout_ref, wup, wdown,
    out_ref, qx, kx, vx, mixed, normed, total,
):
    rows, width = stream_ref.shape
    half = block // 2
    hidden_width = wup.shape[1]
    qx[:half, :] = jnp.zeros((half, width), BF16)
    qx[half : half + rows, :] = q_ref[...]
    qx[half + rows :, :] = jnp.zeros((half, width), BF16)
    for x, own, lane in ((kx, k_ref, 0), (vx, v_ref, width)):
        x[:half, :] = before_ref[:, lane : lane + width]
        x[half : half + rows, :] = own[...]
        x[half + rows :, :] = after_ref[:, lane : lane + width]
    low_lanes = lax.broadcasted_iota(jnp.int32, (block, 128), 1) < HEAD_DIM

    def window(w, carry):
        span = pl.ds(pl.multiple_of(w * block, block), block)
        for pair in range(width // 128):
            lanes = slice(pair * 128, (pair + 1) * 128)
            q, k, v = qx[span, lanes], kx[span, lanes], vx[span, lanes]
            zero = jnp.zeros_like(q)
            both = jnp.concatenate(
                [jnp.where(low_lanes, q, zero), jnp.where(low_lanes, zero, q)], axis=0
            )
            scores = lax.dot_general(
                both, k, (((1,), (1,)), ((), ())), preferred_element_type=F32
            ) * (1.0 / math.sqrt(HEAD_DIM))
            weights = jnp.exp(scores - jnp.max(scores, axis=-1, keepdims=True))
            probs = (weights / jnp.sum(weights, axis=-1, keepdims=True)).astype(BF16)
            out = dot(probs, v)
            mixed[span, lanes] = jnp.where(low_lanes, out[:block], out[block:]).astype(BF16)
        return carry

    lax.fori_loop(0, (rows + block) // block, window, 0, unroll=3)

    step = 256
    for start in range(0, rows, step):
        values = stream_ref[start : start + step, :] + dot(
            mixed[half + start : half + start + step, :], wout_ref[...]
        )
        total[start : start + step, :] = values
        normed[start : start + step, :] = normalize(values)
    chunk = 768
    for i in range(hidden_width // chunk):
        cols = slice(i * chunk, (i + 1) * chunk)
        hidden = jax.nn.gelu(dot(normed[...], wup[:, cols]), approximate=True).astype(BF16)
        total[...] += dot(hidden, wdown[cols, :])
    out_ref[...] = total[...].astype(BF16)


def attend(stream, query, keys, values, before, after, w_out, w_up, w_down, block):
    rows, width = stream.shape
    return pl.pallas_call(
        functools.partial(attend_kernel, block),
        in_specs=[VM] * 9,
        out_specs=VM,
        out_shape=jax.ShapeDtypeStruct((rows, width), BF16),
        scratch_shapes=[pltpu.VMEM((rows + block, width), BF16)] * 4
        + [
            pltpu.VMEM((rows, width), BF16),
            pltpu.VMEM((rows, width), F32),
        ],
        compiler_params=params(16),
        name="attend",
    )(stream, query, keys, values, before, after, w_out, w_up, w_down)


def hold_kernel(from_ref, to_ref, sem):
    copy = pltpu.make_async_copy(from_ref, to_ref, sem)
    copy.start()
    copy.wait()


def hold(array):
    return pl.pallas_call(
        hold_kernel,
        in_specs=[ANY],
        out_specs=VM,
        out_shape=pltpu.VMEM(array.shape, array.dtype),
        scratch_shapes=[pltpu.SemaphoreType.DMA(())],
        compiler_params=params(1),
        name="hold",
    )(array)


def position_kernel(coords_ref, freq_ref, out_ref):
    axes, rows = coords_ref.shape
    places = coords_ref[...].astype(F32)
    places = jnp.concatenate([places, jnp.zeros((8 - axes, rows), F32)], axis=0)
    columns = jnp.transpose(places)
    count = freq_ref.shape[1]
    for a in range(axes):
        angles = columns[:, a : a + 1] * freq_ref[...]
        out_ref[:, 2 * a * count : (2 * a + 1) * count] = jnp.sin(angles)
        out_ref[:, (2 * a + 1) * count : (2 * a + 2) * count] = jnp.cos(angles)


def position_code(places, model_width):
    freq_count = model_width // 6
    frequency = jnp.exp(-math.log(10000.0) * jnp.arange(freq_count, dtype=F32) / freq_count)
    return pl.pallas_call(
        position_kernel,
        in_specs=[VM] * 2,
        out_specs=VM,
        out_shape=jax.ShapeDtypeStruct((places.shape[1], model_width), F32),
        compiler_params=params(16),
        name="position",
    )(places, frequency[None, :])


def share(parts, axis, count, half):
    own, up_first, up_last, down_first, down_last = parts
    up = [(i, (i + 1) % count) for i in range(count)]
    down = [(j, i) for i, j in up]

    def join(a, b):
        return (a.astype(F32) + b[half:].astype(F32)).astype(BF16)

    def move(value, pairs):
        return lax.ppermute(value, axis, pairs)

    from_below = move(up_first, up)
    from_above = move(down_first, down)
    up_last, down_last = join(up_last, from_below), join(down_last, from_above)
    up_last, down_last = move(up_last, up), move(down_last, down)
    return [own, from_below, from_above, up_last, down_last]


def shards(
    features, block_ids, patch_rows, lift_weights, coords, w_in,
    w_query, w_key, w_value, w_out, w_up, w_down,
):
    view_count, segments = lax.axis_size("view"), lax.axis_size("seg")
    rows_here = coords.shape[-1]
    _, _, slots, block, picks = lift_weights.shape
    width = w_in.shape[1]
    quarter = rows_here // block
    half_blocks = quarter // 2

    indices = patch_rows[0].reshape(-1, 128)

    def send(payload):
        return lax.all_to_all(payload, "seg", split_axis=0, concat_axis=0, tiled=True)

    wide = width // 3 * 2
    by_row = jnp.transpose(lift_weights[0], (0, 1, 3, 2))
    first = send(pack(features[0], w_in, indices, segments, 0, wide, block_ids[0].T, by_row))
    second = send(pack(features[0], w_in, indices, segments, wide, width - wide))
    pos = position_code(coords[0, 0], width)
    me = lax.axis_index("view").astype(jnp.int32).reshape(1)
    ids = first[:, slots * picks, slots * 128 : slots * 128 + slots].astype(jnp.int32)

    def sums(rows, counted):
        parts = gather_sums(ids, me, rows, first, block, picks, half_blocks, counted)
        return share(parts, "view", view_count, parts[2].shape[0])

    shares = sums(first, True)
    shares += sums(second, False)
    stream, query, keys, values = project(
        shares, pos, w_query, w_key, w_value, block, half_blocks
    )
    half = block // 2
    device_count = view_count * segments
    ring_up = [(i, (i + 1) % device_count) for i in range(device_count)]
    ring_down = [(j, i) for i, j in ring_up]
    last = jnp.concatenate([keys[rows_here - half :], values[rows_here - half :]], axis=1)
    first = jnp.concatenate([keys[:half], values[:half]], axis=1)
    before = lax.ppermute(last, ("view", "seg"), ring_up)
    after = lax.ppermute(first, ("view", "seg"), ring_down)
    w_down = hold(w_down)
    encoded = attend(stream, query, keys, values, before, after, w_out, w_up, w_down, block)
    return encoded.reshape(1, 1, rows_here, width)


def solution(mesh):
    in_specs = (
        P(("view", "seg"), None, None),
        P(("view", "seg"), None, None),
        P(("view", "seg"), None, None, None),
        P(("view", "seg"), None, None, None, None),
        P("view", "seg", None, None),
        P(),
        P(),
        P(),
        P(),
        P(),
        P(),
        P(),
    )
    out_specs = P("view", "seg", None, None)

    return jax.shard_map(shards, mesh=mesh, in_specs=in_specs, out_specs=out_specs, check_vma=False)
```

```python
import functools
import math

import jax
import jax.numpy as jnp
from jax import lax
from jax.experimental import pallas as pl
from jax.experimental.pallas import tpu as pltpu
from jax.sharding import PartitionSpec as P


HEAD_DIM = 64
F32 = jnp.float32
BF16 = jnp.bfloat16
EXTRA = 16
VM = pl.BlockSpec(memory_space=pltpu.VMEM)
ANY = pl.BlockSpec(memory_space=pl.ANY)


def params(megabytes, **kw):
    return pltpu.CompilerParams(vmem_limit_bytes=megabytes * 1024 * 1024, **kw)


def dot(a, b):
    return lax.dot_general(a, b, (((1,), (0,)), ((), ())), preferred_element_type=F32)


def pack_kernel(start, per_step, weighted, *refs):
    if weighted:
        ids_ref, feat_hbm, win_hbm, idx_ref, lift_ref, out_hbm = refs[:6]
    else:
        feat_hbm, win_hbm, idx_ref, out_hbm = refs[:4]
    feat, win, table, places, packed, feat_sems, win_sem, out_sems = refs[-8:]
    patches = feat.shape[0]
    table_rows, width = table.shape
    segments = packed.shape[0]
    count = per_step * (places.shape[0] // segments)
    each = count // per_step
    row_step = 512

    win_copy = pltpu.make_async_copy(win_hbm.at[:, start : start + width], win, win_sem)
    spans = [slice(s, min(s + row_step, patches)) for s in range(0, patches, row_step)]
    feat_copies = [
        pltpu.make_async_copy(feat_hbm.at[span, :], feat.at[span, :], feat_sems.at[i])
        for i, span in enumerate(spans)
    ]
    win_copy.start()
    for copy in feat_copies:
        copy.start()
    turned = jnp.transpose(idx_ref[...].astype(F32)).astype(jnp.int32)
    for i in range(turned.shape[1]):
        places[i * 128 : (i + 1) * 128, :] = turned[:, i : i + 1]
    table[spans[-1].start :, :] = jnp.zeros((table_rows - spans[-1].start, width), BF16)

    if weighted:
        slots, depth, block = lift_ref.shape[1:]
        line = slots * block
        lane = lax.broadcasted_iota(jnp.int32, (depth, line), 1) // EXTRA
        pickers = lax.broadcasted_iota(jnp.int32, (EXTRA, line), 1) % EXTRA
        pickers = (pickers == lax.broadcasted_iota(jnp.int32, (EXTRA, line), 0)).astype(F32).astype(BF16)
        mark_lane = lax.broadcasted_iota(jnp.int32, (EXTRA, width - 2 * line), 1)

        def weigh(segment, carry):
            both = jnp.concatenate([lift_ref[segment, c] for c in range(slots)], axis=1)
            zero = jnp.zeros_like(both)
            apart = jnp.concatenate(
                [jnp.where(lane == g, both, zero) for g in range(line // EXTRA)], axis=0
            )
            packed[segment, each:, : 2 * line] = lax.dot_general(
                pickers, apart, (((1,), (1,)), ((), ())), preferred_element_type=F32
            ).astype(BF16)
            marks = jnp.zeros(mark_lane.shape, jnp.int32)
            for c in range(slots):
                marks = jnp.where(mark_lane == c, ids_ref[c, segment], marks)
            packed[segment, each:, 2 * line :] = marks.astype(F32).astype(BF16)
            return carry

        lax.fori_loop(0, segments, weigh, 0, unroll=8)

    win_copy.wait()
    weights = win[...].astype(BF16)
    for copy, span in zip(feat_copies, spans):
        copy.wait()
        table[span, :] = dot(feat[span, :], weights).astype(BF16)

    def out_copy(base):
        own = pl.ds(base * per_step, per_step)
        return pltpu.make_async_copy(packed.at[own], out_hbm.at[own], out_sems.at[base])

    def pick(base, carry):
        spot = places[pl.ds(pl.multiple_of(base * count, count), count), :]
        picked = lax.broadcasted_iota(jnp.int32, (count, table_rows), 1) == spot
        rows = dot(picked.astype(F32).astype(BF16), table[...]).astype(BF16)
        for i in range(per_step):
            packed[base * per_step + i, :each, :] = rows[i * each : (i + 1) * each, :]
        out_copy(base).start()
        return carry

    steps = segments // per_step
    lax.fori_loop(0, steps, pick, 0, unroll=True)
    for base in range(steps):
        out_copy(base).wait()


def pack(features, w_in, indices, segments, start, width, ids=None, lift=None):
    patches, channels = features.shape
    count = indices.shape[0] * indices.shape[1]
    per_step = 8
    weighted = lift is not None
    rows = count // segments + (EXTRA if weighted else 0)
    operands, in_specs = [features, w_in, indices], [ANY, ANY, VM]
    if weighted:
        operands = [ids] + operands + [lift]
        in_specs = [pl.BlockSpec(memory_space=pltpu.SMEM)] + in_specs + [VM]
    return pl.pallas_call(
        functools.partial(pack_kernel, start, per_step, weighted),
        in_specs=in_specs,
        out_specs=ANY,
        scratch_shapes=[
            pltpu.VMEM((patches, channels), BF16),
            pltpu.VMEM((channels, width), F32),
            pltpu.VMEM((-(-patches // 128) * 128, width), BF16),
            pltpu.VMEM((count, 1), jnp.int32),
            pltpu.VMEM((segments, rows, width), BF16),
            pltpu.SemaphoreType.DMA((-(-patches // 512),)),
            pltpu.SemaphoreType.DMA(()),
            pltpu.SemaphoreType.DMA((segments // per_step,)),
        ],
        out_shape=jax.ShapeDtypeStruct((segments, rows, width), BF16),
        compiler_params=params(60),
        name="pack",
    )(*operands)


def gather_sums_kernel(block, picks, half_blocks, counted, ids_ref, me_ref, rows_ref, weight_ref, *rest):
    outs, total, stage, sems = rest[-8:-3], rest[-3], rest[-2], rest[-1]
    step = pl.program_id(0)
    views, _, width = rows_ref.shape

    @pl.when(step == 0)
    def _():
        total[...] = jnp.zeros_like(total)

    slots = ids_ref.shape[1]
    size = outs[2].shape[0]
    parts = 8
    depth = slots * picks * 4
    group = lax.broadcasted_iota(jnp.int32, (EXTRA, depth), 1) // picks
    me = me_ref[0]

    def add_view(j, carry):
        weights = weight_ref[j, :, :depth]
        zero = jnp.zeros_like(weights)
        left = jnp.concatenate([jnp.where(group == r, weights, zero) for r in range(slots * 4)], axis=0)
        rows = [rows_ref[j, c * picks : (c + 1) * picks, :] for c in range(slots)]
        right = jnp.concatenate([rows[c] for c in range(slots) for _ in range(4)], axis=0)
        lifted = dot(left, right)
        for c in range(slots):
            name = ids_ref[step * views + j, c]
            owner = name // (2 * half_blocks)
            within = name - owner * (2 * half_blocks)
            half = within // half_blocks
            within = within - half * half_blocks
            away = owner - me + jnp.where(owner < me, parts // 2, 0)
            start = (away * 2 + half) * size
            empty = name == parts * half_blocks
            place = jnp.where(empty, parts * size, start + within * block)
            place = pl.multiple_of(place, 8)
            total[pl.ds(place, block), :] += lifted[c * block : (c + 1) * block, :]
            if counted:
                mark = jnp.where(empty, parts * size + block, start + half_blocks * block + within)
                total[pl.ds(mark, 1), :] += jnp.ones((1, width), F32)
        return carry

    lax.fori_loop(0, views, add_view, 0, unroll=8)

    @pl.when(step == pl.num_programs(0) - 1)
    def _():
        own, up_first, up_last, down_first, down_last = outs
        order = (
            (up_first, 0, 1, 1), (up_first, 1, 2, 0), (down_first, 0, 3, 0), (down_first, 1, 2, 1),
            (up_last, 0, 1, 0), (down_last, 0, 3, 1), (own, 0, 0, 0), (own, 1, 0, 1),
        )
        copies = []
        for i, (out, place, away, half) in enumerate(order):
            first = (away * 2 + half) * size
            stage[i] = total[first : first + size, :].astype(BF16)
            copies.append(
                pltpu.make_async_copy(
                    stage.at[i], out.at[place * size : (place + 1) * size, :], sems.at[i]
                )
            )
            copies[-1].start()
        for copy in copies:
            copy.wait()


def gather_sums(ids, me, rows, weights, block, picks, half_blocks, counted):
    views, _, width = rows.shape
    count = ids.shape[1] * picks
    size = half_blocks * block + (8 if counted else 0)
    sizes = [2 * size, 2 * size, size, 2 * size, size]
    return pl.pallas_call(
        functools.partial(gather_sums_kernel, block, picks, half_blocks, counted),
        grid_spec=pltpu.PrefetchScalarGridSpec(
            num_scalar_prefetch=2,
            grid=(views // 8,),
            in_specs=[
                pl.BlockSpec((8, count, width), lambda i, *_: (i, 0, 0)),
                pl.BlockSpec((8, EXTRA, weights.shape[2]), lambda i, *_: (i, count // EXTRA, 0)),
            ],
            out_specs=[pl.BlockSpec(memory_space=pltpu.HBM)] * len(sizes),
            scratch_shapes=[
                pltpu.VMEM((8 * size + block + 8, width), F32),
                pltpu.VMEM((8, size, width), BF16),
                pltpu.SemaphoreType.DMA((8,)),
            ],
        ),
        out_shape=[
            (pltpu.HBM if counted and i in (0, 2, 4) else jax.ShapeDtypeStruct)((s, width), BF16)
            for i, s in enumerate(sizes)
        ],
        compiler_params=params(20, dimension_semantics=("arbitrary",)),
        name="gather_sums",
    )(ids, me, rows, weights)


def normalize(values):
    average = jnp.mean(values, axis=-1, keepdims=True)
    centred = values - average
    spread = jnp.mean(centred * centred, axis=-1, keepdims=True)
    return (centred * lax.rsqrt(spread + 1e-05)).astype(BF16)


def project_kernel(block, half_blocks, *refs):
    sums = (refs[0:5], refs[5:10])
    pos_ref, wq_ref, wk_ref, wv_ref, stream_ref, q_ref, k_ref, v_ref = refs[10:]
    half_rows = half_blocks * block
    for h in range(2):
        base = h * half_rows

        def load(column, lo, hi):
            own, below_first, above_first, below_last, above_last = sums[column]
            size = below_last.shape[0]
            first, last = (above_first, below_last) if h == 0 else (below_first, above_last)
            here = slice(h * size + lo, h * size + hi)
            return own[here, :].astype(F32) + first[lo:hi, :].astype(F32) + last[lo:hi, :].astype(F32)

        tally = jnp.maximum(load(0, half_rows, half_rows + 8), 1.0)
        for i in range(half_blocks):
            lo = i * block
            for column in range(2):
                start = sums[0][0].shape[1] * column
                lanes = slice(start, start + sums[column][0].shape[1])
                averaged = load(column, lo, lo + block) / tally[i : i + 1, : lanes.stop - lanes.start]
                stream_ref[base + lo : base + lo + block, lanes] = (
                    averaged + pos_ref[base + lo : base + lo + block, lanes]
                )
        normed = normalize(stream_ref[base : base + half_rows, :])
        for w_ref, o_ref in ((wk_ref, k_ref), (wv_ref, v_ref), (wq_ref, q_ref)):
            o_ref[base : base + half_rows, :] = dot(normed, w_ref[...]).astype(BF16)


def project(sums, pos, w_query, w_key, w_value, block, half_blocks):
    rows, width = pos.shape
    return pl.pallas_call(
        functools.partial(project_kernel, block, half_blocks),
        in_specs=[VM] * (len(sums) + 4),
        out_specs=[VM] * 4,
        out_shape=[jax.ShapeDtypeStruct((rows, width), F32)]
        + [jax.ShapeDtypeStruct((rows, width), BF16)] * 3,
        compiler_params=params(16),
        cost_estimate=pl.CostEstimate(flops=6 * rows * width * width, bytes_accessed=12 * rows * width, transcendentals=0),
        name="project",
    )(*sums, pos, w_query, w_key, w_value)


def attend_kernel(
    block, stream_ref, q_ref, k_ref, v_ref, before_ref, after_ref, wout_ref, wup, wdown,
    out_ref, qx, kx, vx, mixed, normed, total,
):
    rows, width = stream_ref.shape
    half = block // 2
    hidden_width = wup.shape[1]
    qx[:half, :] = jnp.zeros((half, width), BF16)
    qx[half : half + rows, :] = q_ref[...]
    qx[half + rows :, :] = jnp.zeros((half, width), BF16)
    for x, own, lane in ((kx, k_ref, 0), (vx, v_ref, width)):
        x[:half, :] = before_ref[:, lane : lane + width]
        x[half : half + rows, :] = own[...]
        x[half + rows :, :] = after_ref[:, lane : lane + width]
    low_lanes = lax.broadcasted_iota(jnp.int32, (block, 128), 1) < HEAD_DIM

    def window(w, carry):
        span = pl.ds(pl.multiple_of(w * block, block), block)
        for pair in range(width // 128):
            lanes = slice(pair * 128, (pair + 1) * 128)
            q, k, v = qx[span, lanes], kx[span, lanes], vx[span, lanes]
            zero = jnp.zeros_like(q)
            both = jnp.concatenate(
                [jnp.where(low_lanes, q, zero), jnp.where(low_lanes, zero, q)], axis=0
            )
            scores = lax.dot_general(
                both, k, (((1,), (1,)), ((), ())), preferred_element_type=F32
            ) * (1.0 / math.sqrt(HEAD_DIM))
            weights = jnp.exp(scores - jnp.max(scores, axis=-1, keepdims=True))
            probs = (weights * (1.0 / jnp.sum(weights, axis=-1, keepdims=True))).astype(BF16)
            out = dot(probs, v)
            mixed[span, lanes] = jnp.where(low_lanes, out[:block], out[block:]).astype(BF16)
        return carry

    lax.fori_loop(0, (rows + block) // block, window, 0, unroll=True)

    step = 256
    for start in range(0, rows, step):
        values = stream_ref[start : start + step, :] + dot(
            mixed[half + start : half + start + step, :], wout_ref[...]
        )
        total[start : start + step, :] = values
        normed[start : start + step, :] = normalize(values)
    chunk = 1536
    for i in range(hidden_width // chunk):
        cols = slice(i * chunk, (i + 1) * chunk)
        hidden = jax.nn.gelu(dot(normed[...], wup[:, cols]), approximate=True).astype(BF16)
        if i < hidden_width // chunk - 1:
            total[...] += dot(hidden, wdown[cols, :])
        else:
            out_ref[...] = (total[...] + dot(hidden, wdown[cols, :])).astype(BF16)


def attend(stream, query, keys, values, before, after, w_out, w_up, w_down, block):
    rows, width = stream.shape
    return pl.pallas_call(
        functools.partial(attend_kernel, block),
        in_specs=[VM] * 9,
        out_specs=VM,
        out_shape=jax.ShapeDtypeStruct((rows, width), BF16),
        scratch_shapes=[pltpu.VMEM((rows + block, width), BF16)] * 4
        + [
            pltpu.VMEM((rows, width), BF16),
            pltpu.VMEM((rows, width), F32),
        ],
        compiler_params=params(16),
        name="attend",
    )(stream, query, keys, values, before, after, w_out, w_up, w_down)


def hold_kernel(from_ref, to_ref, sem):
    copy = pltpu.make_async_copy(from_ref, to_ref, sem)
    copy.start()
    copy.wait()


def hold(array):
    return pl.pallas_call(
        hold_kernel,
        in_specs=[ANY],
        out_specs=VM,
        out_shape=pltpu.VMEM(array.shape, array.dtype),
        scratch_shapes=[pltpu.SemaphoreType.DMA(())],
        compiler_params=params(1),
        name="hold",
    )(array)


def position_kernel(coords_ref, freq_ref, out_ref):
    axes, rows = coords_ref.shape
    places = coords_ref[...].astype(F32)
    places = jnp.concatenate([places, jnp.zeros((8 - axes, rows), F32)], axis=0)
    columns = jnp.transpose(places)
    count = freq_ref.shape[1]
    for a in range(axes):
        angles = columns[:, a : a + 1] * freq_ref[...]
        out_ref[:, 2 * a * count : (2 * a + 1) * count] = jnp.sin(angles)
        out_ref[:, (2 * a + 1) * count : (2 * a + 2) * count] = jnp.cos(angles)


def position_code(places, model_width):
    freq_count = model_width // 6
    frequency = jnp.exp(-math.log(10000.0) * jnp.arange(freq_count, dtype=F32) / freq_count)
    return pl.pallas_call(
        position_kernel,
        in_specs=[VM] * 2,
        out_specs=VM,
        out_shape=jax.ShapeDtypeStruct((places.shape[1], model_width), F32),
        compiler_params=params(16),
        name="position",
    )(places, frequency[None, :])


def share(parts, axis, count, half):
    own, up_first, up_last, down_first, down_last = parts
    up = [(i, (i + 1) % count) for i in range(count)]
    down = [(j, i) for i, j in up]

    def join(a, b):
        return (a.astype(F32) + b[half:].astype(F32)).astype(BF16)

    def move(value, pairs):
        return lax.ppermute(value, axis, pairs)

    from_below = move(up_first, up)
    from_above = move(down_first, down)
    up_last, down_last = join(up_last, from_below), join(down_last, from_above)
    up_last, down_last = move(up_last, up), move(down_last, down)
    return [own, from_below, from_above, up_last, down_last]


def shards(
    features, block_ids, patch_rows, lift_weights, coords, w_in,
    w_query, w_key, w_value, w_out, w_up, w_down,
):
    view_count, segments = lax.axis_size("view"), lax.axis_size("seg")
    rows_here = coords.shape[-1]
    _, _, slots, block, picks = lift_weights.shape
    width = w_in.shape[1]
    quarter = rows_here // block
    half_blocks = quarter // 2

    indices = patch_rows[0].reshape(-1, 128)

    def send(payload):
        return lax.all_to_all(payload, "seg", split_axis=0, concat_axis=0, tiled=True)

    wide = width // 3 * 2
    by_row = jnp.transpose(lift_weights[0], (0, 1, 3, 2))
    first = send(pack(features[0], w_in, indices, segments, 0, wide, block_ids[0].T, by_row))
    second = send(pack(features[0], w_in, indices, segments, wide, width - wide))
    pos = position_code(coords[0, 0], width)
    me = lax.axis_index("view").astype(jnp.int32).reshape(1)
    ids = first[:, slots * picks, slots * 128 : slots * 128 + slots].astype(jnp.int32)

    def sums(rows, counted):
        parts = gather_sums(ids, me, rows, first, block, picks, half_blocks, counted)
        return share(parts, "view", view_count, parts[2].shape[0])

    shares = sums(first, True)
    shares += sums(second, False)
    stream, query, keys, values = project(
        shares, pos, w_query, w_key, w_value, block, half_blocks
    )
    half = block // 2
    device_count = view_count * segments
    ring_up = [(i, (i + 1) % device_count) for i in range(device_count)]
    ring_down = [(j, i) for i, j in ring_up]
    last = jnp.concatenate([keys[rows_here - half :], values[rows_here - half :]], axis=1)
    first = jnp.concatenate([keys[:half], values[:half]], axis=1)
    before = lax.ppermute(last, ("view", "seg"), ring_up)
    after = lax.ppermute(first, ("view", "seg"), ring_down)
    w_down = hold(w_down)
    encoded = attend(stream, query, keys, values, before, after, w_out, w_up, w_down, block)
    return encoded.reshape(1, 1, rows_here, width)


def solution(mesh):
    in_specs = (
        P(("view", "seg"), None, None),
        P(("view", "seg"), None, None),
        P(("view", "seg"), None, None, None),
        P(("view", "seg"), None, None, None, None),
        P("view", "seg", None, None),
        P(),
        P(),
        P(),
        P(),
        P(),
        P(),
        P(),
    )
    out_specs = P("view", "seg", None, None)

    return jax.shard_map(shards, mesh=mesh, in_specs=in_specs, out_specs=out_specs, check_vma=False)
```
